32 devices in a mesh: chan: 4 (over y, x), rows: 8 (over z, core).
Axes of the slice: x: 2, y: 2, z: 4, core: 2. Of those that a mesh axis runs over, the one named last changes fastest.
Arguments:
- inputs: bfloat16 [49152, 512], P('rows', 'chan'), may hold values from -6 to 6
- cotangent: bfloat16 [49152, 512], P('rows', 'chan'), may hold values from -6 to 6
- top_index: int32 [512, 8, 25], P('rows'), may hold values from 0 to 95, as said below
- attention_weight: float32 [4, 262144], P(None, ('chan', 'rows')), as said below
- attention_first: float32 [4, 262144], P(None, ('chan', 'rows')), may hold values from -1280 to 1280
- attention_second: float32 [4, 262144], P(None, ('chan', 'rows')), may hold values from 12288 to 196608
- feed_weight: float32 [2, 1048576], P(None, ('chan', 'rows')), as said below
- feed_first: float32 [2, 1048576], P(None, ('chan', 'rows')), may hold values from -1280 to 1280
- feed_second: float32 [2, 1048576], P(None, ('chan', 'rows')), may hold values from 12288 to 196608
- vector_params: float32 [12, 512], replicated, as said below
- vector_first: float32 [12, 512], replicated, may hold values from -1280 to 1280
- vector_second: float32 [12, 512], replicated, may hold values from 12288 to 196608
Outputs:
- encoded: bfloat16 [49152, 512], P('rows', 'chan')
- input_grad: bfloat16 [49152, 512], P('rows', 'chan')
- attention_grad: float32 [4, 262144], P(None, ('chan', 'rows'))
- feed_grad: float32 [2, 1048576], P(None, ('chan', 'rows'))
- vector_grad: float32 [12, 512], replicated
- attention_first_new: float32 [4, 262144], P(None, ('chan', 'rows'))
- attention_second_new: float32 [4, 262144], P(None, ('chan', 'rows'))
- feed_first_new: float32 [2, 1048576], P(None, ('chan', 'rows'))
- feed_second_new: float32 [2, 1048576], P(None, ('chan', 'rows'))
- vector_first_new: float32 [12, 512], replicated
- vector_second_new: float32 [12, 512], replicated
- attention_new: float32 [4, 262144], P(None, ('chan', 'rows'))
- feed_new: float32 [2, 1048576], P(None, ('chan', 'rows'))
- vector_new: float32 [12, 512], replicated
- attention_copy: bfloat16 [4, 262144], P(None, ('chan', 'rows'))
- feed_copy: bfloat16 [2, 1048576], P(None, ('chan', 'rows'))
- matrix_norms: float32 [6, 2], replicated
The draws below stay inside these ranges and needn't reach their ends.
Inputs may be any that keep to these rules, and one draw needn't show every extreme that they name: `top_index`: each window and head names 25 different positions. `attention_weight`: real entries. `feed_weight`: real entries. `vector_params`: real entries.
All inputs are finite; a program needn't handle non-finite values.
Results may differ from the reference program's by a relative error of at most 0.012.
The reference program's roundings to bfloat16 on the way count: a program that leaves them out, or rounds other values in their place, can miss the bound.
Values may be sent and summed in bfloat16 or wider, within the bound.
A program may use at most 128 MiB of HBM per device.

```python
import math
import jax
import jax.numpy as jnp
from jax import lax

D = 512
H = 8
FF = 2048
L = 96
U = 25
STEP = 3
SEQS = 512
TOKENS = 49152


def draw_top_index(key, part):
    scores = jax.random.randint(key, (SEQS, H, L), 0, 1048576) * L + jnp.arange(L, dtype=jnp.int32)
    return jnp.argsort(scores, axis=-1)[..., :U].astype(jnp.int32)


def draw_attention_weight(key, part):
    noise = jax.random.normal(key, (4, D * D), jnp.float32)
    spread = jnp.where(jnp.arange(4)[:, None] == 3, (L / D) ** 0.5, D ** (-0.5))
    return noise * spread


def draw_feed_weight(key, part):
    noise = jax.random.normal(key, (2, D * FF), jnp.float32)
    spread = jnp.where(jnp.arange(2)[:, None] == 0, D ** (-0.5), FF ** (-0.5))
    return noise * spread


def draw_vector_params(key, part):
    noise = 0.3 * jax.random.normal(key, (12, D), jnp.float32)
    row_index = jnp.arange(12)[:, None]
    gain_row = (row_index == 8) | (row_index == 10)
    return jnp.where(gain_row, 1.0 + noise, noise)


def steps_of(rng, shape, split, least, high):
    factor_of = 1.0
    for axis_at, parts in split:
        steps = jax.random.uniform(jax.random.fold_in(jax.random.fold_in(rng, 6), axis_at), (parts,), jnp.float32, least / len(split), high / len(split))
        factor_of = factor_of * jnp.repeat(jnp.exp(steps), shape[axis_at] // parts).reshape((-1,) + (1,) * (len(shape) - 1 - axis_at))
    return factor_of


def centred(key, extent, deviation, limit, cuts=(), held_as=jnp.bfloat16):
    array = deviation * jax.random.normal(key, extent, jnp.float32)
    if cuts:
        array = array * steps_of(key, extent, cuts, -0.22, 0.18)
    return jnp.clip(array, -limit, limit).astype(held_as)


def setup_inputs(seed: int = 0) -> dict:
    streams_of = jax.random.split(jax.random.key(seed), 13)
    inputs = centred(streams_of[0], (TOKENS, D), 1.0, 6.0, ((0, 8), (1, 4)))
    cotangent = centred(streams_of[1], (TOKENS, D), 1.0, 6.0, ((0, 8), (1, 4)))
    top_index = draw_top_index(jax.random.fold_in(streams_of[12], 71), 0)
    attention_weight = draw_attention_weight(jax.random.fold_in(streams_of[12], 71), 0)
    attention_first = centred(streams_of[4], (4, D * D), (TOKENS ** 0.5), 1280.0, ((1, 32),), jnp.float32)
    attention_second = jnp.clip(jnp.exp(math.log(196608.0) - 2.7725887 * jax.random.uniform(streams_of[5], (4, D * D), jnp.float32) ** steps_of(streams_of[5], (4, D * D), ((1, 32),), -0.2, 0.2)), 12288.0, 196608.0)
    feed_weight = draw_feed_weight(jax.random.fold_in(streams_of[12], 71), 0)
    feed_first = centred(streams_of[7], (2, D * FF), (TOKENS ** 0.5), 1280.0, ((1, 32),), jnp.float32)
    feed_second = jnp.clip(jnp.exp(math.log(196608.0) - 2.7725887 * jax.random.uniform(streams_of[8], (2, D * FF), jnp.float32) ** steps_of(streams_of[8], (2, D * FF), ((1, 32),), -0.2, 0.2)), 12288.0, 196608.0)
    vector_params = draw_vector_params(jax.random.fold_in(streams_of[12], 71), 0)
    vector_first = centred(streams_of[10], (12, D), (TOKENS ** 0.5), 1280.0, (), jnp.float32)
    vector_second = jnp.clip(jnp.exp(jax.random.uniform(streams_of[11], (12, D), jnp.float32, math.log(12288.0), math.log(196608.0))), 12288.0, 196608.0)
    return {"inputs": inputs, "cotangent": cotangent, "top_index": top_index, "attention_weight": attention_weight, "attention_first": attention_first, "attention_second": attention_second, "feed_weight": feed_weight, "feed_first": feed_first, "feed_second": feed_second, "vector_params": vector_params, "vector_first": vector_first, "vector_second": vector_second}


@jax.custom_vjp
def low(v):
    return lax.optimization_barrier(v.astype(jnp.bfloat16)).astype(jnp.float32)

@jax.custom_vjp
def low_back(v):
    return v

def low_keep(v):
    return (low(v), None)

def low_pass(kept, grad):
    return (grad,)

def back_keep(v):
    return (v, None)

def back_low(kept, grad):
    return (low(grad),)
low.defvjp(low_keep, low_pass)
low_back.defvjp(back_keep, back_low)
HIGHEST = lax.Precision.HIGHEST
norm_epsilon = 1e-05
epsilon = 1e-06
beta_first = 0.5
beta_second = 0.5
learn_rate = 0.3
weight_decay = 0.01
root_half = 0.7071067811865476

def matmul(matrix_a, matrix_b):
    return jnp.dot(matrix_a, matrix_b, precision=HIGHEST)

def normalize(values):
    centered = values - lax.optimization_barrier(jnp.mean(values, axis=-1, keepdims=True))
    variance = lax.optimization_barrier(jnp.mean(centered * centered, axis=-1, keepdims=True))
    return centered * lax.rsqrt(variance + norm_epsilon)

def gelu_exact(values):
    return 0.5 * values * (1.0 + jax.scipy.special.erf(values * root_half))

def block_forward(params, rows, chosen):
    w_query, w_key, w_value, w_output, w_inner, w_outer, vectors = params
    groups = chosen.shape[0]
    head_size = D // H
    query = low(low_back(matmul(rows, w_query) + vectors[4])).reshape(groups, L, H, head_size)
    keys = low(low_back(matmul(rows, w_key))).reshape(groups, L, H, head_size)
    values = low(low_back(matmul(rows, w_value) + vectors[5])).reshape(groups, L, H, head_size)
    select = (chosen[..., None] == jnp.arange(L, dtype=jnp.int32)).astype(jnp.float32)
    picked = jnp.einsum('ghul,glhd->ghud', select, query, precision=HIGHEST)
    scores = low_back(jnp.einsum('ghud,glhd->ghul', picked, keys, precision=HIGHEST) * head_size ** (-0.5))
    exponent = jnp.exp(scores)
    soft = low(exponent / lax.optimization_barrier(jnp.sum(exponent, axis=-1, keepdims=True)))
    attended = low_back(jnp.einsum('ghul,glhd->ghud', soft, values, precision=HIGHEST))
    mean_fill = lax.optimization_barrier(jnp.mean(values, axis=1))
    context = mean_fill[:, None] + jnp.einsum('ghul,ghud->glhd', select, attended - mean_fill[:, :, None, :], precision=HIGHEST)
    context = low(context.reshape(groups * L, D))
    branch = low_back(matmul(context, w_output) + vectors[6])
    first = normalize(rows + branch) * vectors[8] + vectors[9]
    inner = low_back(matmul(low(first), w_inner) + vectors[0:4].reshape(-1))
    outer = low_back(matmul(low(gelu_exact(inner)), w_outer) + vectors[7])
    return normalize(first + outer) * vectors[10] + vectors[11]

def lamb_rows(weight, grad, first, second):
    first_new = beta_first * first + (1.0 - beta_first) * grad
    second_new = beta_second * second + (1.0 - beta_second) * grad * grad
    update = first_new / (1.0 - beta_first ** STEP) / (jnp.sqrt(second_new / (1.0 - beta_second ** STEP)) + epsilon) + weight_decay * weight
    weight_sq = lax.optimization_barrier(jnp.sum(weight * weight, axis=-1))
    update_sq = lax.optimization_barrier(jnp.sum(update * update, axis=-1))
    ratio = jnp.sqrt(weight_sq) * lax.rsqrt(update_sq + epsilon)
    new_weight = weight - learn_rate * ratio[:, None] * update
    norms = jnp.stack([jnp.sqrt(weight_sq), jnp.sqrt(update_sq)], axis=-1)
    return (first_new, second_new, new_weight, norms)

def reference(inputs, cotangent, top_index, attention_weight, attention_first, attention_second, feed_weight, feed_first, feed_second, vector_params, vector_first, vector_second):
    group = math.gcd(SEQS, 32)
    blocks = SEQS // group
    rows_all = inputs.astype(jnp.float32).reshape(blocks, group * L, D)
    chosen_all = top_index.reshape(blocks, group, H, U)

    def forward(rows_in, attention_w, feed_w, vectors):
        params = (low(attention_w[0].reshape(D, D)), low(attention_w[1].reshape(D, D)), low(attention_w[2].reshape(D, D)), low(attention_w[3].reshape(D, D)), low(feed_w[0].reshape(D, FF)), low(feed_w[1].reshape(FF, D)), vectors)
        block_step = jax.checkpoint(lambda rows, chosen: block_forward(params, rows, chosen))
        return lax.map(lambda pair: block_step(pair[0], pair[1]), (rows_in, chosen_all))
    encoded, pullback = jax.vjp(forward, rows_all, attention_weight, feed_weight, vector_params)
    grad_rows, attention_grad, feed_grad, vector_grad = pullback(cotangent.astype(jnp.float32).reshape(blocks, group * L, D))
    attention_first_new, attention_second_new, attention_new, attention_norms = lamb_rows(attention_weight, attention_grad, attention_first, attention_second)
    feed_first_new, feed_second_new, feed_new, feed_norms = lamb_rows(feed_weight, feed_grad, feed_first, feed_second)
    vector_first_new, vector_second_new, vector_new, unused = lamb_rows(vector_params, vector_grad, vector_first, vector_second)
    matrix_norms = jnp.concatenate([attention_norms, feed_norms], axis=0)
    return (encoded.reshape(TOKENS, D).astype(jnp.bfloat16), grad_rows.reshape(TOKENS, D).astype(jnp.bfloat16), attention_grad, feed_grad, vector_grad, attention_first_new, attention_second_new, feed_first_new, feed_second_new, vector_first_new, vector_second_new, attention_new, feed_new, vector_new, attention_new.astype(jnp.bfloat16), feed_new.astype(jnp.bfloat16), matrix_norms)
```

```python
import functools
import jax
import jax.numpy as jnp
from jax import lax
from jax.experimental import pallas as pl
from jax.experimental.pallas import tpu as pltpu
from jax.sharding import PartitionSpec as P

STEP = 3
HIGHEST = lax.Precision.HIGHEST
norm_epsilon = 1e-05
epsilon = 1e-06
beta_first = 0.5
beta_second = 0.5
learn_rate = 0.3
weight_decay = 0.01
root_half = 0.7071067811865476
inverse_root_tau = 0.3989422804014327


bf=jnp.bfloat16; f32=jnp.float32
L=96; H=8
EPS=1e-5
def _dg(a,b,ca,cb): return lax.dot_general(a,b,(((ca,),(cb,)),((),())),preferred_element_type=f32)
def nn(a,b): return _dg(a,b,1,0)
def nt(a,b): return _dg(a,b,1,1)
def tn(a,b): return _dg(a,b,0,0)

def lane_iota(shape): return lax.broadcasted_iota(jnp.int32,shape,1)

def gelu_both(F):
    ph = 0.5*(1.0+lax.erf(F*0.7071067811865476))
    pdf = jnp.exp(-0.5*F*F)*0.3989422804014327
    return F*ph, ph+F*pdf

def pick_mask(idx_ref, w, mk_ref):
    it = lax.broadcasted_iota(jnp.int32,(L,H),0)
    m = jnp.zeros((L,H),f32)
    blk = idx_ref[w]
    for j in range(25):
        m = jnp.where(it==blk[j:j+1,:],1.0,m)
    mk_ref[pl.ds(pl.multiple_of(w*L,L),L),:]=m

def fill_bd(bd_ref, s, val):
    li = lane_iota((L,128))
    z = jnp.zeros((L,128),bf)
    for h in range(H):
        p=h//2
        blk=val[:,p*128:(p+1)*128]
        blk=jnp.where((li<64) if h%2==0 else (li>=64), blk, z)
        bd_ref[s,h*128:h*128+L,(p%2)*128:(p%2)*128+128]=blk

SC=64**-0.5
def attn_fwd(s,q,k,v,m8,kbd,vbd,ab_ref,r0):
    fill_bd(kbd,s,k); fill_bd(vbd,s,v)
    li = lane_iota((L,128))
    mean = jnp.sum(v.astype(f32),axis=0,keepdims=True)*(1.0/L)
    outs=[]
    for g in range(2):
        S = nt(q[:,g*256:(g+1)*256],kbd[s,g*512:(g+1)*512,:])
        abs_=[]; mb=[]
        for hh in range(4):
            h=g*4+hh
            mh=jnp.broadcast_to(m8[:,h:h+1],(L,128))>0.5
            mb.append(mh)
            sh=jnp.where(mh,S[:,hh*128:(hh+1)*128]*SC,0.0)
            e=jnp.where(li<L,jnp.exp(sh),0.0)
            r=jnp.sum(e,axis=1,keepdims=True)
            a=e*(1.0/r)
            abs_.append(jnp.where(mh,a,0.0).astype(bf))
        ab=jnp.concatenate(abs_,axis=1)
        ab_ref[pl.ds(r0,L),g*512:(g+1)*512]=ab
        O=nn(ab,vbd[s,g*512:(g+1)*512,:])
        for pp in range(2):
            mlo=jnp.where(mb[2*pp],1.0,0.0); mhi=jnp.where(mb[2*pp+1],1.0,0.0)
            msk=jnp.where(li<64,mlo,mhi)>0.5
            c0=g*256+pp*128
            outs.append(jnp.where(msk,O[:,pp*128:(pp+1)*128],mean[:,c0:c0+128]))
    return jnp.concatenate(outs,axis=1).astype(bf)

def attn_bwd(s,q,k,v,ab,dC,m8,kbd,vbd):
    fill_bd(kbd,s,k); fill_bd(vbd,s,v)
    li = lane_iota((L,128))
    msks=[]
    for p in range(4):
        mlo=jnp.broadcast_to(m8[:,2*p:2*p+1],(L,128)); mhi=jnp.broadcast_to(m8[:,2*p+1:2*p+2],(L,128))
        msks.append(jnp.where(li<64,mlo,mhi))
    msk=jnp.concatenate(msks,axis=1)>0.5
    dO=jnp.where(msk,dC,0.0).astype(bf)
    dM=jnp.sum(jnp.where(msk,0.0,dC),axis=0,keepdims=True)*(1.0/L)
    dqs=[];dks=[];dvs=[]
    for g in range(2):
        c=slice(g*256,(g+1)*256)
        dA=nt(dO[:,c],vbd[s,g*512:(g+1)*512,:])
        dss=[]
        for hh in range(4):
            h=g*4+hh
            a=ab[:,h*128:(h+1)*128].astype(f32)
            da=dA[:,hh*128:(hh+1)*128]
            t=a*da
            r=jnp.sum(t,axis=1,keepdims=True)
            dss.append((t-a*r).astype(bf))
        dS=jnp.concatenate(dss,axis=1)
        dqs.append(nn(dS,kbd[s,g*512:(g+1)*512,:])*SC)
        TK=tn(dS,q[:,c])
        TV=tn(ab[:,g*512:(g+1)*512],dO[:,c])
        for pp in range(2):
            h0=2*pp*128; h1=h0+128; cs=slice(pp*128,(pp+1)*128)
            dks.append(jnp.where(li<64,TK[h0:h0+L,cs],TK[h1:h1+L,cs])*SC)
            dvs.append(jnp.where(li<64,TV[h0:h0+L,cs],TV[h1:h1+L,cs]))
    dQ=jnp.concatenate(dqs,axis=1).astype(bf)
    dK=jnp.concatenate(dks,axis=1).astype(bf)
    dV=(jnp.concatenate(dvs,axis=1)+dM).astype(bf)
    return dQ,dK,dV

def norm_parts(r):
    cen=r-jnp.mean(r,axis=-1,keepdims=True)
    var=jnp.mean(cen*cen,axis=-1,keepdims=True)
    rs=lax.rsqrt(var+EPS)
    return cen*rs,rs
def norm_back(gh,n,rs):
    return rs*(gh-jnp.mean(gh,axis=-1,keepdims=True)-n*jnp.mean(gh*n,axis=-1,keepdims=True))

def csum(x): return jnp.sum(x,axis=0,keepdims=True)

def p1(R, PW=2):
    x,idx,wq,wk,wv,wo,vec=R['x'],R['idx'],R['wq'],R['wk'],R['wv'],R['wo'],R['vec']
    T=x.shape[0]; TM=PW*L
    R['kbd'][...]=jnp.zeros_like(R['kbd']); R['vbd'][...]=jnp.zeros_like(R['vbd'])
    @pl.loop(0,T//L)
    def _(w): pick_mask(idx,w,R['mk'])
    @pl.loop(0,T//TM)
    def _(i):
        r0=pl.multiple_of(i*TM,TM)
        rows=pl.ds(r0,TM)
        xb=x[rows,:]
        q=(nn(xb,wq[...])+vec[4:5,:]).astype(bf)
        k=nn(xb,wk[...]).astype(bf)
        v=(nn(xb,wv[...])+vec[5:6,:]).astype(bf)
        R['q'][rows,:]=q; R['k'][rows,:]=k; R['v'][rows,:]=v
        cs=[]
        for s in range(PW):
            sl=slice(s*L,(s+1)*L)
            r1=pl.multiple_of(r0+s*L,L)
            cs.append(attn_fwd(s,q[sl],k[sl],v[sl],R['mk'][pl.ds(r1,L),:],R['kbd'],R['vbd'],R['ab'],r1))
        c=jnp.concatenate(cs,axis=0)
        R['c'][rows,:]=c
        rr=xb.astype(f32)+(nn(c,wo[...])+vec[6:7,:])
        n,rs=norm_parts(rr)
        R['n1h'][rows,:]=n
        R['rs1'][rows,:]=rs
        R['n1b'][rows,:]=(n*vec[8:9,:]+vec[9:10,:]).astype(bf)

def p2(R,TM=256,JB=512):
    vec,w1,w2,cot,b1=R['vec'],R['w1'],R['w2'],R['cot'],R['b1']
    T=cot.shape[0]; FFW=w1.shape[1]
    gv=R['gv']; gb1=R['gb1']
    gv[...]=jnp.zeros_like(gv); gb1[...]=jnp.zeros_like(gb1)
    @pl.loop(0,T//TM)
    def _(i):
        r0=pl.multiple_of(i*TM,TM); rows=pl.ds(r0,TM)
        n1h=R['n1h'][rows,:]
        n1b=R['n1b'][rows,:]
        acc=n1h*vec[8:9,:]+vec[9:10,:]+vec[7:8,:]
        for j in range(FFW//JB):
            js=slice(j*JB,(j+1)*JB)
            F=nn(n1b,w1[:,js])+b1[:,js]
            G,sl=gelu_both(F)
            G=G.astype(bf)
            R['g'][rows,js]=G
            R['sl'][:,js]=sl.astype(bf)
            acc=acc+nn(G,w2[js,:])
        yh,rs2=norm_parts(acc)
        R['y'][rows,:]=(yh*vec[10:11,:]+vec[11:12,:]).astype(bf)
        dY=cot[rows,:].astype(f32)
        gv[6:7,:]+=csum(dY*yh); gv[7:8,:]+=csum(dY)
        dR2=norm_back(dY*vec[10:11,:],yh,rs2)
        dZ=dR2.astype(bf)
        R['dz'][rows,:]=dZ
        gv[3:4,:]+=csum(dZ.astype(f32))
        acc2=dR2
        for j in range(FFW//JB):
            js=slice(j*JB,(j+1)*JB)
            dG=nt(dZ,w2[js,:])
            dF=(dG*R['sl'][:,js].astype(f32)).astype(bf)
            R['df'][rows,js]=dF
            gb1[:,js]+=csum(dF.astype(f32))
            acc2=acc2+nt(dF,w1[:,js])
        n1h=R['n1h'][rows,:]
        gv[4:5,:]+=csum(acc2*n1h); gv[5:6,:]+=csum(acc2)
        dR1=norm_back(acc2*vec[8:9,:],n1h,R['rs1'][rows,:])
        R['n1h'][rows,:]=dR1
        dB=dR1.astype(bf)
        R['db'][rows,:]=dB
        gv[2:3,:]+=csum(dB.astype(f32))

def p3(R,MB=256):
    g,dz,n1b,df,c,db=R['g'],R['dz'],R['n1b'],R['df'],R['c'],R['db']
    FFW=g.shape[1]
    @pl.loop(0,FFW//MB)
    def _(j):
        js=pl.ds(pl.multiple_of(j*MB,MB),MB)
        R['dw2'][js,:]=tn(g[:,js],dz[...]).astype(R['dw2'].dtype)
    @pl.loop(0,FFW//MB)
    def _(j):
        js=pl.ds(pl.multiple_of(j*MB,MB),MB)
        R['dw1'][:,js]=tn(n1b[...],df[:,js]).astype(R['dw1'].dtype)
    @pl.loop(0,512//MB)
    def _(j):
        js=pl.ds(pl.multiple_of(j*MB,MB),MB)
        R['dwo'][js,:]=tn(c[:,js],db[...]).astype(R['dwo'].dtype)

def p4(R,PW=2):
    wq,wk,wv,wo=R['wq'],R['wk'],R['wv'],R['wo']
    gv=R['gv']
    T=R['x'].shape[0]; TM=PW*L
    @pl.loop(0,T//TM)
    def _(i):
        r0=pl.multiple_of(i*TM,TM); rows=pl.ds(r0,TM)
        dC=nt(R['db'][rows,:],wo[...])
        a=[];b=[];d=[]
        for s in range(PW):
            r1=pl.multiple_of(r0+s*L,L); rs=pl.ds(r1,L)
            dq,dk,dv=attn_bwd(s,R['q'][rs,:],R['k'][rs,:],R['v'][rs,:],R['ab'][rs,:],dC[s*L:(s+1)*L],R['mk'][rs,:],R['kbd'],R['vbd'])
            a.append(dq);b.append(dk);d.append(dv)
        dq=jnp.concatenate(a,0);dk=jnp.concatenate(b,0);dv=jnp.concatenate(d,0)
        R['q'][rows,:]=dq;R['k'][rows,:]=dk;R['v'][rows,:]=dv
        gv[0:1,:]+=csum(dq.astype(f32)); gv[1:2,:]+=csum(dv.astype(f32))
        gx=R['n1h'][rows,:]+nt(dq,wq[...])+nt(dk,wk[...])+nt(dv,wv[...])
        R['dx'][rows,:]=gx.astype(bf)

def p5(R,MB=256):
    x=R['x']
    for nm,src in (('dwq','q'),('dwk','k'),('dwv','v')):
        @pl.loop(0,512//MB)
        def _(j):
            js=pl.ds(pl.multiple_of(j*MB,MB),MB)
            R[nm][js,:]=tn(x[:,js],R[src][...]).astype(R[nm].dtype)
INS=['x','cot','idx','wq','wk','wv','wo','w1','w2','vec','b1']
OUTS=['y','dx','dwq','dwk','dwv','dwo','dw1','dw2','gv','gb1']
def scratch(T):
    V=pltpu.VMEM
    return dict(kbd=V((2,1024,256),bf),vbd=V((2,1024,256),bf),mk=V((T,8),f32),q=V((T,512),bf),k=V((T,512),bf),v=V((T,512),bf),
      ab=V((T,1024),bf),c=V((T,512),bf),n1h=V((T,512),f32),rs1=V((T,1),f32),n1b=V((T,512),bf),g=V((T,2048),bf),sl=V((256,2048),bf),
      df=V((T,2048),bf),dz=V((T,512),bf),db=V((T,512),bf))
def compute(args, phases=(1,2,3,4,5), gdt=bf):
    T=args['x'].shape[0]
    sc=scratch(T); names=list(sc)
    def kern(*refs):
        R={}
        for n,r in zip(INS+OUTS+names,refs): R[n]=r
        if 1 in phases: p1(R)
        if 2 in phases: p2(R)
        if 3 in phases: p3(R)
        if 4 in phases: p4(R)
        if 5 in phases: p5(R)
    S=jax.ShapeDtypeStruct
    outs=dict(y=S((T,512),bf),dx=S((T,512),bf),dwq=S((512,512),gdt),dwk=S((512,512),gdt),dwv=S((512,512),gdt),dwo=S((512,512),gdt),
       dw1=S((512,2048),gdt),dw2=S((2048,512),gdt),gv=S((8,512),f32),gb1=S((1,2048),f32))
    vm=pl.BlockSpec(memory_space=pltpu.VMEM)
    r=pl.pallas_call(kern,out_shape=[outs[o] for o in OUTS],in_specs=[vm]*len(INS),out_specs=[vm]*len(OUTS),
       scratch_shapes=[sc[n] for n in names],compiler_params=pltpu.CompilerParams(vmem_limit_bytes=63<<20))(*[args[n] for n in INS])
    return dict(zip(OUTS,r))

def lamb_parts(weight, grad, first, second):
    first_new = beta_first * first + (1.0 - beta_first) * grad
    second_new = beta_second * second + (1.0 - beta_second) * grad * grad
    update = (
        first_new
        / (1.0 - beta_first**STEP)
        / (jnp.sqrt(second_new / (1.0 - beta_second**STEP)) + epsilon)
        + weight_decay * weight
    )
    squares = jnp.stack(
        [jnp.sum(weight * weight, axis=-1), jnp.sum(update * update, axis=-1)], axis=-1
    )
    return (first_new, second_new, update, squares)


def lamb_finish(weight, update, squares):
    ratio = jnp.sqrt(squares[:, 0]) * lax.rsqrt(squares[:, 1] + epsilon)
    return (weight - learn_rate * ratio[:, None] * update, jnp.sqrt(squares))


def local(
    inputs,
    cotangent,
    top_index,
    attention_weight,
    attention_first,
    attention_second,
    feed_weight,
    feed_first,
    feed_second,
    vector_params,
    vector_first,
    vector_second,
):
    rows_in, back_in = (
        lax.all_to_all(inputs, "chan", split_axis=0, concat_axis=1, tiled=True),
        lax.all_to_all(cotangent, "chan", split_axis=0, concat_axis=1, tiled=True),
    )
    model_width = rows_in.shape[1]
    row_total = rows_in.shape[0]
    sequences = row_total // L
    chosen = lax.dynamic_slice_in_dim(top_index, lax.axis_index("chan") * sequences, sequences, 0)
    attention_full, feed_full = (
        lax.all_gather(attention_weight.astype(jnp.bfloat16), ("chan", "rows"), axis=1, tiled=True),
        lax.all_gather(feed_weight.astype(jnp.bfloat16), ("chan", "rows"), axis=1, tiled=True),
    )
    hidden_width = feed_full.shape[1] // model_width
    out = compute(dict(
        x=rows_in, cot=back_in, idx=jnp.swapaxes(chosen, 1, 2),
        wq=attention_full[0].reshape(model_width, model_width),
        wk=attention_full[1].reshape(model_width, model_width),
        wv=attention_full[2].reshape(model_width, model_width),
        wo=attention_full[3].reshape(model_width, model_width),
        w1=feed_full[0].reshape(model_width, hidden_width),
        w2=feed_full[1].reshape(hidden_width, model_width),
        vec=vector_params, b1=vector_params[0:4].reshape(1, -1)), gdt=f32)
    encoded, grad_rows = out["y"], out["dx"]
    encoded_cols, grad_cols = (
        lax.all_to_all(encoded, "chan", split_axis=1, concat_axis=0, tiled=True),
        lax.all_to_all(
            grad_rows, "chan", split_axis=1, concat_axis=0, tiled=True
        ),
    )
    attention_local = jnp.stack([out[n].reshape(-1) for n in ("dwq", "dwk", "dwv", "dwo")], axis=0)
    feed_local = jnp.stack([out[n].reshape(-1) for n in ("dw1", "dw2")], axis=0)
    vector_local = jnp.concatenate([out["gb1"].reshape(-1, model_width), out["gv"]], axis=0)
    attention_grad = lax.psum_scatter(attention_local, ("chan", "rows"), scatter_dimension=1, tiled=True)
    feed_grad = lax.psum_scatter(feed_local, ("chan", "rows"), scatter_dimension=1, tiled=True)
    vector_grad = lax.psum(vector_local, ("chan", "rows"))
    attention_state = lamb_parts(
        attention_weight, attention_grad, attention_first, attention_second
    )
    feed_state = lamb_parts(feed_weight, feed_grad, feed_first, feed_second)
    squares = lax.psum(
        jnp.concatenate([attention_state[3], feed_state[3]], axis=0), ("chan", "rows")
    )
    vector_state = lamb_parts(vector_params, vector_grad, vector_first, vector_second)
    attention_new, attention_norms = lamb_finish(attention_weight, attention_state[2], squares[0:4])
    feed_new, feed_norms = lamb_finish(feed_weight, feed_state[2], squares[4:6])
    vector_new, unused = lamb_finish(vector_params, vector_state[2], vector_state[3])
    matrix_norms = jnp.concatenate([attention_norms, feed_norms], axis=0)
    return (
        encoded_cols,
        grad_cols,
        attention_grad,
        feed_grad,
        vector_grad,
        attention_state[0],
        attention_state[1],
        feed_state[0],
        feed_state[1],
        vector_state[0],
        vector_state[1],
        attention_new,
        feed_new,
        vector_new,
        attention_new.astype(jnp.bfloat16),
        feed_new.astype(jnp.bfloat16),
        matrix_norms,
    )


def solution(mesh):
    in_specs = (
        P("rows", "chan"),
        P("rows", "chan"),
        P("rows", None, None),
        P(None, ("chan", "rows")),
        P(None, ("chan", "rows")),
        P(None, ("chan", "rows")),
        P(None, ("chan", "rows")),
        P(None, ("chan", "rows")),
        P(None, ("chan", "rows")),
        P(),
        P(),
        P(),
    )
    out_specs = (
        P("rows", "chan"),
        P("rows", "chan"),
        P(None, ("chan", "rows")),
        P(None, ("chan", "rows")),
        P(),
        P(None, ("chan", "rows")),
        P(None, ("chan", "rows")),
        P(None, ("chan", "rows")),
        P(None, ("chan", "rows")),
        P(),
        P(),
        P(None, ("chan", "rows")),
        P(None, ("chan", "rows")),
        P(),
        P(None, ("chan", "rows")),
        P(None, ("chan", "rows")),
        P(),
    )
    return jax.shard_map(local, mesh=mesh, in_specs=in_specs, out_specs=out_specs, check_vma=False)
```

```python
import functools

import jax
import jax.numpy as jnp
from jax import lax
from jax.experimental import pallas as pl
from jax.experimental.pallas import tpu as pltpu
from jax.sharding import PartitionSpec as P

STEP = 3
epsilon = 1e-06
beta_first = 0.5
beta_second = 0.5
learn_rate = 0.3
weight_decay = 0.01


bf = jnp.bfloat16
f32 = jnp.float32
L = 96
H = 8
NZ = 4
SC = 0.125
EPS = 1e-5
SDS = jax.ShapeDtypeStruct


def _dg(a, b, ca, cb):
    return lax.dot_general(a, b, (((ca,), (cb,)), ((), ())), preferred_element_type=f32)


def nn(a, b):
    return _dg(a, b, 1, 0)


def nt(a, b):
    return _dg(a, b, 1, 1)


def tn(a, b):
    return _dg(a, b, 0, 0)


def csum(v):
    return jnp.sum(v, axis=0, keepdims=True)


def gelu_both(F):
    ph = 0.5 * (1.0 + lax.erf(F * 0.7071067811865476))
    pdf = jnp.exp(-0.5 * F * F) * 0.3989422804014327
    return F * ph, ph + F * pdf


def norm_parts(r):
    cen = r - jnp.mean(r, axis=-1, keepdims=True)
    var = jnp.mean(cen * cen, axis=-1, keepdims=True)
    rs = lax.rsqrt(var + EPS)
    return cen * rs, rs


def norm_back(gh, n, rs):
    return rs * (gh - jnp.mean(gh, axis=-1, keepdims=True) - n * jnp.mean(gh * n, axis=-1, keepdims=True))


def pick_mask(idx_ref, w, mk_ref):
    it = lax.broadcasted_iota(jnp.int32, (L, H), 0)
    m = jnp.zeros((L, H), f32)
    blk = idx_ref[w]
    for j in range(blk.shape[0]):
        m = jnp.where(it == blk[j : j + 1, :], 1.0, m)
    mk_ref[pl.ds(pl.multiple_of(w * L, L), L), 0:H] = m


def fill_bd(bd_ref, s, val):
    li = lax.broadcasted_iota(jnp.int32, (L, 128), 1)
    z = jnp.zeros((L, 128), bf)
    for h in range(H):
        p = h // 2
        blk = jnp.where((li < 64) if h % 2 == 0 else (li >= 64), val[:, p * 128 : (p + 1) * 128], z)
        bd_ref[s, h * 128 : h * 128 + L, (p % 2) * 128 : (p % 2) * 128 + 128] = blk


def attn_fwd(s, q, k, v, m8, kbd, vbd, ab_ref, r0):
    fill_bd(kbd, s, k)
    fill_bd(vbd, s, v)
    li = lax.broadcasted_iota(jnp.int32, (L, 128), 1)
    mean = csum(v.astype(f32)) * (1.0 / L)
    outs = []
    for g in range(2):
        S = nt(q[:, g * 256 : (g + 1) * 256], kbd[s, g * 512 : (g + 1) * 512, :])
        abs_ = []
        mb = []
        for hh in range(4):
            h = g * 4 + hh
            mh = jnp.broadcast_to(m8[:, h : h + 1], (L, 128))
            mb.append(mh)
            picked = mh > 0.5
            sh = jnp.where(picked, S[:, hh * 128 : (hh + 1) * 128] * SC, 0.0)
            e = jnp.where(li < L, jnp.exp(sh), 0.0)
            r = jnp.sum(e, axis=1, keepdims=True)
            abs_.append(jnp.where(picked, e * (1.0 / r), 0.0).astype(bf))
        ab = jnp.concatenate(abs_, axis=1)
        ab_ref[pl.ds(r0, L), g * 512 : (g + 1) * 512] = ab
        O = nn(ab, vbd[s, g * 512 : (g + 1) * 512, :])
        for pp in range(2):
            msk = jnp.where(li < 64, mb[2 * pp], mb[2 * pp + 1]) > 0.5
            c0 = g * 256 + pp * 128
            outs.append(jnp.where(msk, O[:, pp * 128 : (pp + 1) * 128], mean[:, c0 : c0 + 128]))
    return jnp.concatenate(outs, axis=1).astype(bf)


def attn_bwd(s, q, k, v, ab, dC, m8, kbd, vbd):
    fill_bd(kbd, s, k)
    fill_bd(vbd, s, v)
    li = lax.broadcasted_iota(jnp.int32, (L, 128), 1)
    msks = []
    for p in range(4):
        mlo = jnp.broadcast_to(m8[:, 2 * p : 2 * p + 1], (L, 128))
        mhi = jnp.broadcast_to(m8[:, 2 * p + 1 : 2 * p + 2], (L, 128))
        msks.append(jnp.where(li < 64, mlo, mhi))
    msk = jnp.concatenate(msks, axis=1) > 0.5
    dO = jnp.where(msk, dC, 0.0).astype(bf)
    dM = csum(jnp.where(msk, 0.0, dC)) * (1.0 / L)
    dqs = []
    dks = []
    dvs = []
    for g in range(2):
        c = slice(g * 256, (g + 1) * 256)
        dA = nt(dO[:, c], vbd[s, g * 512 : (g + 1) * 512, :])
        dss = []
        for hh in range(4):
            h = g * 4 + hh
            a = ab[:, h * 128 : (h + 1) * 128].astype(f32)
            t = a * dA[:, hh * 128 : (hh + 1) * 128]
            r = jnp.sum(t, axis=1, keepdims=True)
            dss.append((t - a * r).astype(bf))
        dS = jnp.concatenate(dss, axis=1)
        dqs.append(nn(dS, kbd[s, g * 512 : (g + 1) * 512, :]) * SC)
        TK = tn(dS, q[:, c])
        TV = tn(ab[:, g * 512 : (g + 1) * 512], dO[:, c])
        for pp in range(2):
            h0 = 2 * pp * 128
            h1 = h0 + 128
            cs = slice(pp * 128, (pp + 1) * 128)
            dks.append(jnp.where(li < 64, TK[h0 : h0 + L, cs], TK[h1 : h1 + L, cs]) * SC)
            dvs.append(jnp.where(li < 64, TV[h0 : h0 + L, cs], TV[h1 : h1 + L, cs]))
    dQ = jnp.concatenate(dqs, axis=1).astype(bf)
    dK = jnp.concatenate(dks, axis=1).astype(bf)
    dV = (jnp.concatenate(dvs, axis=1) + dM).astype(bf)
    return dQ, dK, dV


def wmat(R, i):
    v = R["wa"][i]
    return v.reshape(512, 512)


def nohook(i):
    pass


PW = 2
TM1 = PW * L
TM2 = 384
JB = 512
MB = 256


def p0(R):
    R["kbd"][...] = jnp.zeros_like(R["kbd"])
    R["vbd"][...] = jnp.zeros_like(R["vbd"])
    R["gv"][...] = jnp.zeros_like(R["gv"])
    R["gb1"][...] = jnp.zeros_like(R["gb1"])

    @pl.loop(0, R["x"].shape[0] // L)
    def _(w):
        pick_mask(R["idx"], w, R["mk"])


def p1(R, hook=nohook):
    x, vec = R["x"], R["vec"]

    @pl.loop(0, x.shape[0] // TM1)
    def _(i):
        hook(i)
        r0 = pl.multiple_of(i * TM1, TM1)
        rows = pl.ds(r0, TM1)
        xb = x[rows, :]
        q = (nn(xb, wmat(R, 0)) + vec[4:5, :]).astype(bf)
        k = nn(xb, wmat(R, 1)).astype(bf)
        v = (nn(xb, wmat(R, 2)) + vec[5:6, :]).astype(bf)
        R["q"][rows, :] = q
        R["k"][rows, :] = k
        R["v"][rows, :] = v
        cs = []
        for s in range(PW):
            sl = slice(s * L, (s + 1) * L)
            r1 = pl.multiple_of(r0 + s * L, L)
            cs.append(attn_fwd(s, q[sl], k[sl], v[sl], R["mk"][pl.ds(r1, L), 0:H], R["kbd"], R["vbd"], R["ab"], r1))
        c = jnp.concatenate(cs, axis=0)
        R["c"][rows, :] = c
        n, rs = norm_parts(xb.astype(f32) + (nn(c, wmat(R, 3)) + vec[6:7, :]))
        R["n1h"][rows, :] = n
        R["mk"][rows, H : H + 1] = rs
        R["n1b"][rows, :] = (n * vec[8:9, :] + vec[9:10, :]).astype(bf)


def p2(R, hook=nohook, done=nohook):
    vec, w1, w2, cot, b1, gv, gb1 = R["vec"], R["w1"], R["w2"], R["cot"], R["b1"], R["gv"], R["gb1"]
    FFW = b1.shape[1]
    D = vec.shape[1]

    @pl.loop(0, cot.shape[0] // TM2)
    def _(i):
        hook(i)
        r0 = pl.multiple_of(i * TM2, TM2)
        rows = pl.ds(r0, TM2)
        n1b = R["n1b"][rows, :]
        acc = R["n1h"][rows, :] * vec[8:9, :] + vec[9:10, :] + vec[7:8, :]
        for j in range(FFW // JB):
            js = slice(j * JB, (j + 1) * JB)
            F = nn(n1b, w1[:, :, :, :, js].reshape(D, JB)) + b1[:, js]
            G, sl = gelu_both(F)
            G = G.astype(bf)
            R["g"][rows, js] = G
            R["df"][rows, js] = sl.astype(bf)
            acc = acc + nn(G, w2[j].reshape(JB, D))
        yh, rs2 = norm_parts(acc)
        dY = cot[rows, :].astype(f32)
        R["y"][rows, :] = (yh * vec[10:11, :] + vec[11:12, :]).astype(bf)
        done(i)
        gv[6:7, :] += csum(dY * yh)
        gv[7:8, :] += csum(dY)
        dR2 = norm_back(dY * vec[10:11, :], yh, rs2)
        dZ = dR2.astype(bf)
        R["dz"][rows, :] = dZ
        gv[3:4, :] += csum(dZ.astype(f32))
        acc2 = dR2
        for j in range(FFW // JB):
            js = slice(j * JB, (j + 1) * JB)
            dG = nt(dZ, w2[j].reshape(JB, D))
            dF = (dG * R["df"][rows, js].astype(f32)).astype(bf)
            R["df"][rows, js] = dF
            gb1[:, js] += csum(dF.astype(f32))
            acc2 = acc2 + nt(dF, w1[:, :, :, :, js].reshape(D, JB))
        n1h = R["n1h"][rows, :]
        gv[4:5, :] += csum(acc2 * n1h)
        gv[5:6, :] += csum(acc2)
        dR1 = norm_back(acc2 * vec[8:9, :], n1h, R["mk"][rows, H : H + 1])
        R["n1h"][rows, :] = dR1
        dB = dR1.astype(bf)
        R["db"][rows, :] = dB
        gv[2:3, :] += csum(dB.astype(f32))


def p3_w2(R):
    @pl.loop(0, R["g"].shape[1] // MB)
    def _(j):
        js = pl.ds(pl.multiple_of(j * MB, MB), MB)
        r = tn(R["g"][:, js], R["dz"][...]).astype(bf)
        R["g2"][j // 2, pl.ds((j % 2) * 2, 2)] = r.reshape(2, 2, 64, 512)


def p3_w1(R):
    @pl.loop(0, R["g"].shape[1] // MB)
    def _(j):
        js = pl.ds(pl.multiple_of(j * MB, MB), MB)
        r = tn(R["n1b"][...], R["df"][:, js]).astype(bf)
        R["g1"][:, :, :, :, js] = r.reshape(4, NZ, 2, 16, MB)


def grad_attn(R, i, left, right):
    @pl.loop(0, 512 // MB)
    def _(j):
        js = pl.ds(pl.multiple_of(j * MB, MB), MB)
        r = tn(R[left][:, js], R[right][...]).astype(bf)
        R["ga"][i, pl.ds(j * 2, 2)] = r.reshape(2, NZ, 2, 16, 512)


def p4(R, hook=nohook, done=nohook):
    gv = R["gv"]

    @pl.loop(0, R["x"].shape[0] // TM1)
    def _(i):
        hook(i)
        r0 = pl.multiple_of(i * TM1, TM1)
        rows = pl.ds(r0, TM1)
        dC = nt(R["db"][rows, :], wmat(R, 3))
        a = []
        b = []
        d = []
        for s in range(PW):
            rs = pl.ds(pl.multiple_of(r0 + s * L, L), L)
            dq, dk, dv = attn_bwd(
                s, R["q"][rs, :], R["k"][rs, :], R["v"][rs, :], R["ab"][rs, :], dC[s * L : (s + 1) * L],
                R["mk"][rs, 0:H], R["kbd"], R["vbd"],
            )
            a.append(dq)
            b.append(dk)
            d.append(dv)
        dq = jnp.concatenate(a, 0)
        dk = jnp.concatenate(b, 0)
        dv = jnp.concatenate(d, 0)
        R["q"][rows, :] = dq
        R["k"][rows, :] = dk
        R["v"][rows, :] = dv
        gv[0:1, :] += csum(dq.astype(f32))
        gv[1:2, :] += csum(dv.astype(f32))
        gx = R["n1h"][rows, :] + nt(dq, wmat(R, 0)) + nt(dk, wmat(R, 1)) + nt(dv, wmat(R, 2))
        R["dx"][rows, :] = gx.astype(bf)
        done(i)


def scratch_of(T, D, FFW):
    V = pltpu.VMEM
    return dict(
        kbd=V((PW, 1024, 256), bf), vbd=V((PW, 1024, 256), bf), mk=V((T, 16), f32),
        q=V((T, D), bf), k=V((T, D), bf), v=V((T, D), bf), ab=V((T, 1024), bf), c=V((T, D), bf),
        n1h=V((T, D), f32), n1b=V((T, D), bf), g=V((T, FFW), bf), df=V((T, FFW), bf),
        dz=V((T, D), bf), db=V((T, D), bf),
    )


def compute(x, cot, idx, vec, b1, wa, w1, w2):
    T, D = x.shape
    sc = scratch_of(T, D, b1.shape[1])
    ins = ["x", "cot", "idx", "vec", "b1", "wa", "w1", "w2"]
    outs = dict(
        y=SDS((T, D), bf), dx=SDS((T, D), bf), ga=SDS(wa.shape, bf), g1=SDS(w1.shape, bf), g2=SDS(w2.shape, bf),
        gv=SDS((8, D), f32), gb1=SDS(b1.shape, f32),
    )
    names = ins + list(outs) + list(sc)

    def kern(*refs):
        R = dict(zip(names, refs))
        p0(R)
        p1(R)
        p2(R)
        p3_w2(R)
        p3_w1(R)
        grad_attn(R, 3, "c", "db")
        p4(R)
        for i, n in enumerate(("q", "k", "v")):
            grad_attn(R, i, "x", n)

    vm = pl.BlockSpec(memory_space=pltpu.VMEM)
    return pl.pallas_call(
        kern, out_shape=list(outs.values()), in_specs=[vm] * len(ins), out_specs=[vm] * len(outs),
        scratch_shapes=list(sc.values()), compiler_params=pltpu.CompilerParams(vmem_limit_bytes=63 << 20),
    )(x, cot, idx, vec, b1, wa, w1, w2)


MESH = pl.DeviceIdType.MESH
CH = 384


class Copies:
    def __init__(self, ss, rs):
        self.ss, self.rs, self.n = ss, rs, 0
        self.sent = []

    def ids(self, count):
        first = self.n
        self.n += count
        return first

    def make(self, i, src, dst, peer):
        return pltpu.make_async_remote_copy(
            src_ref=src, dst_ref=dst, send_sem=self.ss.at[i], recv_sem=self.rs.at[i], device_id=peer,
            device_id_type=MESH,
        )


N_SEM = 160
N_LOC = 16


def mega(inputs, cotangent, idx, vec, b1, sh_a, sh_1, sh_2):
    T = inputs.shape[0] // 4
    D = vec.shape[1]
    FFW = b1.shape[1]
    NC = T // CH
    V = pltpu.VMEM
    ins = ["xin", "cin", "idx", "vec", "b1", "sh_a", "sh_1", "sh_2"]
    outs = dict(
        yo=SDS(inputs.shape, bf), dxo=SDS(inputs.shape, bf), oa=SDS(sh_a.shape, f32), o1=SDS(sh_1.shape, f32),
        o2=SDS(sh_2.shape, f32), ov=SDS((12, D), f32),
    )
    sc = scratch_of(T, D, FFW)
    sc.update(
        x=V((T, D), bf), cot=V((T, D), bf), wa=V((4, 4, NZ, 2, 16, D), bf), w1=V((4, NZ, 2, 16, FFW), bf),
        w2=V((4, NZ, 2, 64, D), bf), ga=V((4, 4, NZ, 2, 16, D), bf), g1=V((4, NZ, 2, 16, FFW), bf),
        g2=V((4, NZ, 2, 64, D), bf), gv=V((8, D), f32), gb1=V((1, FFW), f32),
        ra0=V((4, 4, NZ, 16, D), bf), r10=V((4, NZ, 16, FFW), bf), r20=V((4, NZ, 64, D), bf),
        rax=V((4, 3, NZ, 16, D), bf), raz=V((4, 3, 16, D), bf),
        r1x=V((3, NZ, 16, FFW), bf), r1z=V((3, 16, FFW), bf),
        r2z=V((3, 4, 64, D), bf), r2x=V((3, 64, D), bf),
        va=V((16, D), f32), vb=V((16, D), f32), vx=V((4, 16, D), f32), vz=V((NZ, 16, D), f32),
        ss=pltpu.SemaphoreType.DMA((N_SEM,)), rs=pltpu.SemaphoreType.DMA((N_SEM,)),
        ls=pltpu.SemaphoreType.DMA((N_LOC,)),
    )
    names = ins + list(outs) + list(sc)

    def kern(*refs):
        R = dict(zip(names, refs))
        R["y"] = R["cot"]
        R["dx"] = R["c"]
        ch = lax.axis_index("chan")
        ro = lax.axis_index("rows")
        z = ro // 2
        c = ro % 2
        o = 1 - c
        px = [(ch ^ d, ro) for d in (1, 2, 3)]
        pz = [(ch, (z ^ d) * 2 + c) for d in (1, 2, 3)]
        pc = (ch, z * 2 + o)
        middle = jnp.logical_or(z == 1, z == 2)
        C = Copies(R["ss"], R["rs"])
        ls = R["ls"]

        def rows_in(src, dst, first):
            def cp(k, d):
                return C.make(
                    first + k * 3 + d - 1, src.at[pl.ds((ch ^ d) * T + k * CH, CH), :],
                    dst.at[pl.ds(k * CH, CH), pl.ds(pl.multiple_of(ch * 128, 128), 128)], px[d - 1],
                )
            return cp

        def rows_out(src, dst, first):
            def cp(k, d):
                return C.make(
                    first + k * 3 + d - 1,
                    src.at[pl.ds(k * CH, CH), pl.ds(pl.multiple_of((ch ^ d) * 128, 128), 128)],
                    dst.at[pl.ds(ch * T + k * CH, CH), :], px[d - 1],
                )
            return cp

        x_cp = rows_in(R["xin"], R["x"], C.ids(3 * NC))
        c_cp = rows_in(R["cin"], R["cot"], C.ids(3 * NC))
        y_cp = rows_out(R["y"], R["yo"], C.ids(3 * NC))
        dx_cp = rows_out(R["dx"], R["dxo"], C.ids(3 * NC))
        DS = (1, 2, 3)
        own = pl.ds(pl.multiple_of(ch * 128, 128), 128)
        x_loc = pltpu.make_async_copy(R["xin"].at[pl.ds(ch * T, T), :], R["x"].at[:, own], ls.at[0])
        c_loc = pltpu.make_async_copy(R["cin"].at[pl.ds(ch * T, T), :], R["cot"].at[:, own], ls.at[1])
        y_loc = pltpu.make_async_copy(R["y"].at[:, own], R["yo"].at[pl.ds(ch * T, T), :], ls.at[2])
        dx_loc = pltpu.make_async_copy(R["dx"].at[:, own], R["dxo"].at[pl.ds(ch * T, T), :], ls.at[3])

        class Gather:
            def __init__(self, shard, loc, place, sets):
                ia, ib, ic, iw = C.ids(3), C.ids(3), C.ids(4), C.ids(1)
                self.loc = pltpu.make_async_copy(shard, place(ch, z, c), ls.at[loc])
                self.plane = [C.make(ia + d - 1, shard, place(ch, z, c), px[d - 1]) for d in DS]
                self.chain = [C.make(ib + d - 1, sets(z, c), sets(z, c), pz[d - 1]) for d in DS]
                self.onward = pltpu.make_async_remote_copy(
                    src_ref=sets(z ^ 2, c), dst_ref=sets(z ^ 2, c), send_sem=C.ss.at[iw], recv_sem=C.rs.at[ib + 2],
                    device_id=pz[0], device_id_type=MESH,
                )
                self.core = [C.make(ic + d, sets(z ^ d, c), sets(z ^ d, c), pc) for d in range(4)]

            def start(self):
                for cp in self.plane:
                    cp.start()
                self.loc.start()

            def along(self):
                self.loc.wait()
                for cp in self.plane:
                    cp.wait_recv()
                for cp in self.chain[:2]:
                    cp.start()

                @pl.when(middle)
                def _():
                    self.chain[2].start()

                self.core[0].start()

            def near(self):
                self.chain[0].wait_recv()
                self.core[1].start()
                self.chain[1].wait_recv()

                @pl.when(middle)
                def _():
                    self.onward.start()

                self.core[2].start()

            def far(self):
                self.chain[2].wait_recv()
                self.core[3].start()

            def arrive(self):
                for cp in self.core:
                    cp.wait_recv()

            def finish(self):
                for cp in self.plane + self.chain[:2] + self.core:
                    cp.wait_send()

                @pl.when(middle)
                def _():
                    self.chain[2].wait_send()
                    self.onward.wait_send()

        wa, w1, w2 = R["wa"], R["w1"], R["w2"]
        GA = Gather(R["sh_a"], 4, lambda a, b, e: wa.at[:, a, b, e], lambda b, e: wa.at[:, :, b, e])
        G1 = Gather(R["sh_1"], 5, lambda a, b, e: w1.at[a, b, e], lambda b, e: w1.at[:, b, e])
        G2 = Gather(R["sh_2"], 6, lambda a, b, e: w2.at[a, b, e], lambda b, e: w2.at[:, b, e])

        class Scatter:
            def __init__(self, g, out, b0, bx, bz, plane_first):
                i0, i1, i2 = C.ids(1), C.ids(3), C.ids(3)
                self.g, self.out, self.b0, self.bx, self.bz, self.plane_first = g, out, b0, bx, bz, plane_first
                self.s0 = C.make(i0, g.at[:, :, o], b0, pc)
                if plane_first:
                    self.s1 = [C.make(i1 + d - 1, g.at[ch ^ d, :, c], bx.at[d - 1], px[d - 1]) for d in DS]
                    self.s2 = [C.make(i2 + d - 1, g.at[ch, z ^ d, c], bz.at[d - 1], pz[d - 1]) for d in DS]
                else:
                    self.s1 = [C.make(i1 + d - 1, g.at[:, z ^ d, c], bz.at[d - 1], pz[d - 1]) for d in DS]
                    self.s2 = [C.make(i2 + d - 1, g.at[ch ^ d, z, c], bx.at[d - 1], px[d - 1]) for d in DS]

            def begin(self):
                self.s0.start()

            def one(self):
                self.s0.wait_recv()
                g = self.g

                @pl.loop(0, 4)
                def _(j):
                    g[j, :, c] = (g[j, :, c].astype(f32) + self.b0[j].astype(f32)).astype(bf)

                for cp in self.s1:
                    cp.start()

            def two(self):
                for cp in self.s1:
                    cp.wait_recv()
                g = self.g
                b = self.bx if self.plane_first else self.bz

                @pl.loop(0, 4)
                def _(j):
                    t = b[0, j].astype(f32) + b[1, j].astype(f32) + b[2, j].astype(f32)
                    if self.plane_first:
                        g[ch, j, c] = (g[ch, j, c].astype(f32) + t).astype(bf)
                    else:
                        g[j, z, c] = (g[j, z, c].astype(f32) + t).astype(bf)

                for cp in self.s2:
                    cp.start()

            def three(self):
                for cp in self.s2:
                    cp.wait_recv()
                b = self.bz if self.plane_first else self.bx
                t = b[0].astype(f32) + b[1].astype(f32) + b[2].astype(f32)
                self.out[...] = self.g[ch, z, c].astype(f32) + t

            def finish(self):
                for cp in [self.s0] + self.s1 + self.s2:
                    cp.wait_send()

        S1 = Scatter(R["g1"], R["o1"], R["r10"], R["r1x"], R["r1z"], True)
        S2 = Scatter(R["g2"], R["o2"], R["r20"], R["r2x"], R["r2z"], False)
        SA = [
            Scatter(R["ga"].at[i], R["oa"].at[i], R["ra0"].at[i], R["rax"].at[i], R["raz"].at[i], True) for i in range(4)
        ]
        va, vb, vx, vz = R["va"], R["vb"], R["vx"], R["vz"]
        iv = C.ids(7)
        v0 = C.make(iv, va, vb, pc)
        v1 = [C.make(iv + d, vx.at[ch], vx.at[ch], px[d - 1]) for d in DS]
        v2 = [C.make(iv + 3 + d, vz.at[z], vz.at[z], pz[d - 1]) for d in DS]
        assert C.n <= N_SEM

        bar = pltpu.get_barrier_semaphore()
        for peer in px + pz + [pc]:
            pl.semaphore_signal(bar, inc=1, device_id=peer, device_id_type=MESH)
        pl.semaphore_wait(bar, 7)

        GA.start()
        x_loc.start()
        for d in DS:
            x_cp(0, d).start()
        G1.start()
        G2.start()

        @pl.loop(1, NC)
        def _(k):
            for d in DS:
                x_cp(k, d).start()

        c_loc.start()
        p0(R)
        GA.along()
        G1.along()
        G2.along()
        GA.near()
        GA.far()
        GA.arrive()
        x_loc.wait()

        def hook1(i):
            @pl.when(i % 2 == 0)
            def _():
                k = i // 2
                for d in DS:
                    x_cp(k, d).wait_recv()
                for d in DS:
                    c_cp(k, d).start()

            @pl.when(i == 4)
            def _():
                G1.near()

            @pl.when(i == 7)
            def _():
                G1.far()
                G2.near()

        p1(R, hook1)
        G2.far()
        c_loc.wait()
        G1.arrive()
        G2.arrive()

        def hook2(i):
            for d in DS:
                c_cp(i, d).wait_recv()

        def done2(i):
            for d in DS:
                y_cp(i, d).start()

        p2(R, hook2, done2)
        y_loc.start()
        p3_w2(R)
        S2.begin()
        p3_w1(R)
        S2.one()
        S1.begin()
        grad_attn(R, 3, "c", "db")
        S1.one()
        SA[3].begin()

        def hook4(i):
            @pl.when(i == 1)
            def _():
                SA[3].one()

            @pl.when(i == 6)
            def _():
                S1.two()

        def done4(i):
            @pl.when(i % 2 == 1)
            def _():
                for d in DS:
                    dx_cp(i // 2, d).start()

        p4(R, hook4, done4)
        dx_loc.start()
        va[4:12, :] = R["gv"][...]
        for j in range(4):
            va[j : j + 1, :] = R["gb1"][:, j * D : (j + 1) * D]
        va[12:16, :] = jnp.zeros((4, D), f32)
        v0.start()
        S2.two()
        SA[3].two()
        for i, n in enumerate(("q", "k", "v")):
            grad_attn(R, i, "x", n)
            SA[i].begin()
        v0.wait_recv()
        vx[ch] = va[...] + vb[...]
        for cp in v1:
            cp.start()
        for i in range(3):
            SA[i].one()
        for cp in v1:
            cp.wait_recv()
        vz[z] = vx[0] + vx[1] + vx[2] + vx[3]
        for cp in v2:
            cp.start()
        S1.three()
        S2.three()
        for i in range(3):
            SA[i].two()
        SA[3].three()
        for cp in v2:
            cp.wait_recv()
        tot = vz[0] + vz[1] + vz[2] + vz[3]
        R["ov"][...] = tot[0:12, :]
        for i in range(3):
            SA[i].three()

        @pl.loop(0, NC)
        def _(k):
            for d in DS:
                y_cp(k, d).wait_recv()
                dx_cp(k, d).wait_recv()
                x_cp(k, d).wait_send()
                c_cp(k, d).wait_send()
                y_cp(k, d).wait_send()
                dx_cp(k, d).wait_send()

        y_loc.wait()
        dx_loc.wait()
        for t in (GA, G1, G2, S1, S2, *SA):
            t.finish()
        for cp in [v0] + v1 + v2:
            cp.wait_send()

    vm = pl.BlockSpec(memory_space=pltpu.VMEM)
    an = pl.BlockSpec(memory_space=pl.ANY)
    return pl.pallas_call(
        kern, out_shape=list(outs.values()), in_specs=[an, an, vm, vm, vm, an, an, an],
        out_specs=[an, an, vm, vm, vm, vm], scratch_shapes=list(sc.values()),
        compiler_params=pltpu.CompilerParams(
            vmem_limit_bytes=63 << 20, collective_id=0, has_side_effects=True
        ),
    )(inputs, cotangent, idx, vec, b1, sh_a, sh_1, sh_2)


def sum_all(v):
    def kern(v_ref, o_ref, b, vx, vz, ss, rs):
        ch = lax.axis_index("chan")
        ro = lax.axis_index("rows")
        z = ro // 2
        c = ro % 2
        px = [(ch ^ d, ro) for d in (1, 2, 3)]
        pz = [(ch, (z ^ d) * 2 + c) for d in (1, 2, 3)]
        pc = (ch, z * 2 + 1 - c)
        bar = pltpu.get_barrier_semaphore()
        for peer in px + pz + [pc]:
            pl.semaphore_signal(bar, inc=1, device_id=peer, device_id_type=MESH)
        pl.semaphore_wait(bar, 7)
        C = Copies(ss, rs)
        c0 = C.make(0, v_ref, b, pc)
        c1 = [C.make(d, vx.at[ch], vx.at[ch], px[d - 1]) for d in (1, 2, 3)]
        c2 = [C.make(3 + d, vz.at[z], vz.at[z], pz[d - 1]) for d in (1, 2, 3)]
        c0.start()
        c0.wait_recv()
        vx[ch] = v_ref[...] + b[...]
        for cp in c1:
            cp.start()
        for cp in c1:
            cp.wait_recv()
        vz[z] = vx[0] + vx[1] + vx[2] + vx[3]
        for cp in c2:
            cp.start()
        for cp in c2:
            cp.wait_recv()
        o_ref[...] = vz[0] + vz[1] + vz[2] + vz[3]
        for cp in [c0] + c1 + c2:
            cp.wait_send()

    vm = pl.BlockSpec(memory_space=pltpu.VMEM)
    return pl.pallas_call(
        kern, out_shape=SDS(v.shape, f32), in_specs=[vm], out_specs=vm,
        scratch_shapes=[
            pltpu.VMEM(v.shape, f32), pltpu.VMEM((4,) + v.shape, f32), pltpu.VMEM((NZ,) + v.shape, f32),
            pltpu.SemaphoreType.DMA((7,)), pltpu.SemaphoreType.DMA((7,)),
        ],
        compiler_params=pltpu.CompilerParams(collective_id=1, has_side_effects=True),
    )(v)


def lamb_parts(weight, grad, first, second):
    first_new = beta_first * first + (1.0 - beta_first) * grad
    second_new = beta_second * second + (1.0 - beta_second) * grad * grad
    update = (
        first_new
        / (1.0 - beta_first**STEP)
        / (jnp.sqrt(second_new / (1.0 - beta_second**STEP)) + epsilon)
        + weight_decay * weight
    )
    squares = jnp.stack(
        [jnp.sum(weight * weight, axis=-1), jnp.sum(update * update, axis=-1)], axis=-1
    )
    return (first_new, second_new, update, squares)


def lamb_finish(weight, update, squares):
    ratio = jnp.sqrt(squares[:, 0]) * lax.rsqrt(squares[:, 1] + epsilon)
    return (weight - learn_rate * ratio[:, None] * update, jnp.sqrt(squares))


def native(inputs, cotangent, chosen, attention_weight, feed_weight, vec):
    axes = ("chan", "rows")
    D = vec.shape[1]
    x = lax.all_to_all(inputs, "chan", split_axis=0, concat_axis=1, tiled=True)
    cot = lax.all_to_all(cotangent, "chan", split_axis=0, concat_axis=1, tiled=True)
    wa = lax.all_gather(attention_weight.astype(bf), axes, axis=1, tiled=True)
    wf = lax.all_gather(feed_weight.astype(bf), axes, axis=1, tiled=True)
    y, dx, ga, g1, g2, gv, gb1 = compute(
        x, cot, chosen, vec, vec[0:4].reshape(1, -1), wa.reshape(4, 4, NZ, 2, 16, D),
        wf[0].reshape(4, NZ, 2, 16, -1), wf[1].reshape(4, NZ, 2, 64, D),
    )
    yo = lax.all_to_all(y, "chan", split_axis=1, concat_axis=0, tiled=True)
    dxo = lax.all_to_all(dx, "chan", split_axis=1, concat_axis=0, tiled=True)
    ga = ga.reshape(4, -1).astype(f32)
    gf = jnp.stack([g1.reshape(-1), g2.reshape(-1)]).astype(f32)
    ga = lax.psum_scatter(ga, axes, scatter_dimension=1, tiled=True)
    gf = lax.psum_scatter(gf, axes, scatter_dimension=1, tiled=True)
    gv = lax.psum(jnp.concatenate([gb1.reshape(4, D), gv], axis=0), axes)
    return yo, dxo, ga, gf, gv, lambda v: lax.psum(v, axes)


def direct(inputs, cotangent, chosen, attention_weight, feed_weight, vec):
    D = vec.shape[1]
    FFW = 4 * D
    wf = feed_weight.astype(bf)
    yo, dxo, oa, o1, o2, ov = mega(
        inputs, cotangent, chosen, vec, vec[0:4].reshape(1, -1), attention_weight.astype(bf).reshape(4, 16, D),
        wf[0].reshape(16, FFW), wf[1].reshape(64, D),
    )
    gf = jnp.stack([o1.reshape(-1), o2.reshape(-1)])

    def total(v):
        pad = jnp.zeros((8, 128), f32).at[0:6, 0:2].set(v)
        return sum_all(pad)[0:6, 0:2]

    return yo, dxo, oa.reshape(4, -1), gf, ov, total


def step(
    move,
    inputs,
    cotangent,
    top_index,
    attention_weight,
    attention_first,
    attention_second,
    feed_weight,
    feed_first,
    feed_second,
    vector_params,
    vector_first,
    vector_second,
):
    sequences = top_index.shape[0] // 4
    chosen = lax.dynamic_slice_in_dim(top_index, lax.axis_index("chan") * sequences, sequences, 0)
    encoded, grad_cols, attention_grad, feed_grad, vector_grad, total = move(
        inputs, cotangent, jnp.swapaxes(chosen, 1, 2), attention_weight, feed_weight, vector_params
    )
    attention_state = lamb_parts(attention_weight, attention_grad, attention_first, attention_second)
    feed_state = lamb_parts(feed_weight, feed_grad, feed_first, feed_second)
    squares = total(jnp.concatenate([attention_state[3], feed_state[3]], axis=0))
    vector_state = lamb_parts(vector_params, vector_grad, vector_first, vector_second)
    attention_new, attention_norms = lamb_finish(attention_weight, attention_state[2], squares[0:4])
    feed_new, feed_norms = lamb_finish(feed_weight, feed_state[2], squares[4:6])
    vector_new, unused = lamb_finish(vector_params, vector_state[2], vector_state[3])
    matrix_norms = jnp.concatenate([attention_norms, feed_norms], axis=0)
    return (
        encoded,
        grad_cols,
        attention_grad,
        feed_grad,
        vector_grad,
        attention_state[0],
        attention_state[1],
        feed_state[0],
        feed_state[1],
        vector_state[0],
        vector_state[1],
        attention_new,
        feed_new,
        vector_new,
        attention_new.astype(jnp.bfloat16),
        feed_new.astype(jnp.bfloat16),
        matrix_norms,
    )


def solution(mesh):
    small = mesh.shape["chan"] == 4 and mesh.shape["rows"] == 2 * NZ
    local = functools.partial(step, direct if small else native)
    in_specs = (
        P("rows", "chan"),
        P("rows", "chan"),
        P("rows", None, None),
        P(None, ("chan", "rows")),
        P(None, ("chan", "rows")),
        P(None, ("chan", "rows")),
        P(None, ("chan", "rows")),
        P(None, ("chan", "rows")),
        P(None, ("chan", "rows")),
        P(),
        P(),
        P(),
    )
    out_specs = (
        P("rows", "chan"),
        P("rows", "chan"),
        P(None, ("chan", "rows")),
        P(None, ("chan", "rows")),
        P(),
        P(None, ("chan", "rows")),
        P(None, ("chan", "rows")),
        P(None, ("chan", "rows")),
        P(None, ("chan", "rows")),
        P(),
        P(),
        P(None, ("chan", "rows")),
        P(None, ("chan", "rows")),
        P(),
        P(None, ("chan", "rows")),
        P(None, ("chan", "rows")),
        P(),
    )
    return jax.shard_map(local, mesh=mesh, in_specs=in_specs, out_specs=out_specs, check_vma=False)
```

```python
import functools

import jax
import jax.numpy as jnp
from jax import lax
from jax.experimental import pallas as pl
from jax.experimental.pallas import tpu as pltpu
from jax.sharding import PartitionSpec as P

STEP = 3
epsilon = 1e-06
beta_first = 0.5
beta_second = 0.5
learn_rate = 0.3
weight_decay = 0.01


bf = jnp.bfloat16
f32 = jnp.float32
L = 96
H = 8
NZ = 4
SC = 0.125
EPS = 1e-5
SDS = jax.ShapeDtypeStruct


def _dg(a, b, ca, cb):
    return lax.dot_general(a, b, (((ca,), (cb,)), ((), ())), preferred_element_type=f32)


def nn(a, b):
    return _dg(a, b, 1, 0)


def nt(a, b):
    return _dg(a, b, 1, 1)


def tn(a, b):
    return _dg(a, b, 0, 0)


def csum(v):
    return jnp.sum(v, axis=0, keepdims=True)


def gelu_both(F):
    ph = 0.5 * (1.0 + lax.erf(F * 0.7071067811865476))
    pdf = jnp.exp(-0.5 * F * F) * 0.3989422804014327
    return F * ph, ph + F * pdf


def norm_parts(r):
    cen = r - jnp.mean(r, axis=-1, keepdims=True)
    var = jnp.mean(cen * cen, axis=-1, keepdims=True)
    rs = lax.rsqrt(var + EPS)
    return cen * rs, rs


def norm_back(gh, n, rs):
    return rs * (gh - jnp.mean(gh, axis=-1, keepdims=True) - n * jnp.mean(gh * n, axis=-1, keepdims=True))


def pick_mask(idx, lane, w, mk_ref):
    n = idx.shape[1]
    one = (lax.broadcasted_iota(jnp.int32, (n, 128), 0) == lane).astype(bf)
    pos = nn(idx, one)
    li = lax.broadcasted_iota(jnp.int32, (H, 128), 1).astype(f32)
    m = jnp.zeros((H, 128), f32)
    for j in range(idx.shape[0] // H):
        m = jnp.where(li == pos[j * H : (j + 1) * H, :], 1.0, m)
    mk_ref[pl.ds(pl.multiple_of(w * L, L), L), 0:H] = jnp.transpose(m)[0:L, :]


def fill_bd(bd, val):
    li = lax.broadcasted_iota(jnp.int32, (L, 128), 1)
    z = jnp.zeros((L, 128), bf)
    for h in range(H):
        p = h // 2
        blk = jnp.where((li < 64) if h % 2 == 0 else (li >= 64), val[:, p * 128 : (p + 1) * 128], z)
        bd[h * 128 : h * 128 + L, (p % 2) * 128 : (p % 2) * 128 + 128] = blk


def attn_fwd(q, k, v, m8, kbd, vbd, ab_ref, r0):
    fill_bd(kbd, k)
    fill_bd(vbd, v)
    li = lax.broadcasted_iota(jnp.int32, (L, 128), 1)
    mean = csum(v.astype(f32)) * (1.0 / L)
    outs = []
    for g in range(2):
        S = nt(q[:, g * 256 : (g + 1) * 256], kbd[g * 512 : (g + 1) * 512, :])
        abs_ = []
        mb = []
        for hh in range(4):
            h = g * 4 + hh
            mh = jnp.broadcast_to(m8[:, h : h + 1], (L, 128))
            mb.append(mh)
            picked = mh > 0.5
            sh = jnp.where(picked, S[:, hh * 128 : (hh + 1) * 128] * SC, 0.0)
            e = jnp.where(li < L, jnp.exp(sh), 0.0)
            r = jnp.sum(e, axis=1, keepdims=True)
            abs_.append(jnp.where(picked, e * (1.0 / r), 0.0).astype(bf))
        ab = jnp.concatenate(abs_, axis=1)
        ab_ref[pl.ds(r0, L), g * 512 : (g + 1) * 512] = ab
        O = nn(ab, vbd[g * 512 : (g + 1) * 512, :])
        for pp in range(2):
            msk = jnp.where(li < 64, mb[2 * pp], mb[2 * pp + 1]) > 0.5
            c0 = g * 256 + pp * 128
            outs.append(jnp.where(msk, O[:, pp * 128 : (pp + 1) * 128], mean[:, c0 : c0 + 128]))
    return jnp.concatenate(outs, axis=1).astype(bf)


def heads_down(blocks):
    z = jnp.zeros((128 - L, 128), bf)
    return jnp.concatenate([jnp.transpose(jnp.concatenate([b, z], 0))[0:L] for b in blocks], axis=1)


def attn_bwd(q, k, v, ab, dC, m8, kbd, vbd, qbd, obd):
    fill_bd(kbd, k)
    fill_bd(vbd, v)
    fill_bd(qbd, q)
    li = lax.broadcasted_iota(jnp.int32, (L, 128), 1)
    msks = []
    for p in range(4):
        mlo = jnp.broadcast_to(m8[:, 2 * p : 2 * p + 1], (L, 128))
        mhi = jnp.broadcast_to(m8[:, 2 * p + 1 : 2 * p + 2], (L, 128))
        msks.append(jnp.where(li < 64, mlo, mhi))
    msk = jnp.concatenate(msks, axis=1) > 0.5
    dO = jnp.where(msk, dC, 0.0).astype(bf)
    fill_bd(obd, dO)
    dM = csum(jnp.where(msk, 0.0, dC)) * (1.0 / L)
    dqs = []
    dks = []
    dvs = []
    for g in range(2):
        c = slice(g * 256, (g + 1) * 256)
        dA = nt(dO[:, c], vbd[g * 512 : (g + 1) * 512, :])
        dss = []
        for hh in range(4):
            h = g * 4 + hh
            a = ab[:, h * 128 : (h + 1) * 128].astype(f32)
            t = a * dA[:, hh * 128 : (hh + 1) * 128]
            r = jnp.sum(t, axis=1, keepdims=True)
            dss.append((t - a * r).astype(bf))
        dS = jnp.concatenate(dss, axis=1)
        dqs.append(nn(dS, kbd[g * 512 : (g + 1) * 512, :]) * SC)
        half = slice(g * 512, (g + 1) * 512)
        dks.append(nn(heads_down(dss), qbd[half, :]) * SC)
        dvs.append(nn(heads_down([ab[:, h * 128 : (h + 1) * 128] for h in range(g * 4, g * 4 + 4)]), obd[half, :]))
    dQ = jnp.concatenate(dqs, axis=1).astype(bf)
    dK = jnp.concatenate(dks, axis=1).astype(bf)
    dV = (jnp.concatenate(dvs, axis=1) + dM).astype(bf)
    return dQ, dK, dV


def wmat(R, i):
    v = R["wa"][i]
    return v.reshape(512, 512)


def nohook(i):
    pass


PW = 4
TM1 = PW * L
TMF = 512
TM2 = 384
TMB = 512
JB = 512
MB = 256


def p0(R, first):
    R["kbd"][...] = jnp.zeros_like(R["kbd"])
    R["vbd"][...] = jnp.zeros_like(R["vbd"])
    R["gv"][...] = jnp.zeros_like(R["gv"])
    R["gb1"][...] = jnp.zeros_like(R["gb1"])
    D = R["vec"].shape[1]
    for j in range(4):
        R["b1"][:, j * D : (j + 1) * D] = R["vec"][j : j + 1, :]

    @pl.loop(0, R["x"].shape[0] // L)
    def _(w):
        n = R["idx"].shape
        idx = R["idx"][...].astype(f32).reshape(n[0] * n[1], n[2]).astype(bf)
        pick_mask(idx, first + w, w, R["mk"])


def p1(R, hook=nohook):
    x, vec = R["x"], R["vec"]

    @pl.loop(0, x.shape[0] // TM1)
    def _(i):
        hook(i)
        r0 = pl.multiple_of(i * TM1, TM1)
        rows = pl.ds(r0, TM1)
        xb = x[rows, :]
        q = (nn(xb, wmat(R, 0)) + vec[4:5, :]).astype(bf)
        k = nn(xb, wmat(R, 1)).astype(bf)
        v = (nn(xb, wmat(R, 2)) + vec[5:6, :]).astype(bf)
        R["q"][rows, :] = q
        R["k"][rows, :] = k
        R["v"][rows, :] = v
        cs = []
        for s in range(PW):
            sl = slice(s * L, (s + 1) * L)
            r1 = pl.multiple_of(r0 + s * L, L)
            cs.append(
                attn_fwd(
                    q[sl], k[sl], v[sl], R["mk"][pl.ds(r1, L), 0:H], R["kbd"].at[s], R["vbd"].at[s], R["ab"], r1
                )
            )
        c = jnp.concatenate(cs, axis=0)
        R["c"][rows, :] = c
        n, rs = norm_parts(xb.astype(f32) + (nn(c, wmat(R, 3)) + vec[6:7, :]))
        R["n1h"][rows, :] = n
        R["mk"][rows, H : H + 1] = rs
        R["n1b"][rows, :] = (n * vec[8:9, :] + vec[9:10, :]).astype(bf)


def p2_inner(R, hook=nohook):
    w1, b1 = R["w1"], R["b1"]
    D = R["vec"].shape[1]

    @pl.loop(0, R["x"].shape[0] // TMF)
    def _(i):
        hook(i)
        rows = pl.ds(pl.multiple_of(i * TMF, TMF), TMF)
        n1b = R["n1b"][rows, :]
        for j in range(b1.shape[1] // JB):
            js = slice(j * JB, (j + 1) * JB)
            G, sl = gelu_both(nn(n1b, w1[:, :, :, :, js].reshape(D, JB)) + b1[:, js])
            R["g"][rows, js] = G.astype(bf)
            R["df"][rows, js] = sl.astype(bf)


def p2_outer(R, hook=nohook, done=nohook):
    vec, w2, cot, gv = R["vec"], R["w2"], R["cot"], R["gv"]
    D = vec.shape[1]
    FFW = R["b1"].shape[1]

    @pl.loop(0, cot.shape[0] // TM2)
    def _(i):
        hook(i)
        rows = pl.ds(pl.multiple_of(i * TM2, TM2), TM2)
        acc = R["n1h"][rows, :] * vec[8:9, :] + vec[9:10, :] + vec[7:8, :]
        acc = acc + nn(R["g"][rows, :], w2[...].reshape(FFW, D))
        yh, rs2 = norm_parts(acc)
        dY = cot[rows, :].astype(f32)
        R["y"][rows, :] = (yh * vec[10:11, :] + vec[11:12, :]).astype(bf)
        done(i)
        gv[6:7, :] += csum(dY * yh)
        gv[7:8, :] += csum(dY)
        dR2 = norm_back(dY * vec[10:11, :], yh, rs2)
        R["dr2"][rows, :] = dR2
        dZ = dR2.astype(bf)
        R["dz"][rows, :] = dZ
        gv[3:4, :] += csum(dZ.astype(f32))


def p2_back(R, hook=nohook):
    vec, w1, w2, gv, gb1 = R["vec"], R["w1"], R["w2"], R["gv"], R["gb1"]
    D = vec.shape[1]

    @pl.loop(0, R["x"].shape[0] // TMB)
    def _(i):
        hook(i)
        rows = pl.ds(pl.multiple_of(i * TMB, TMB), TMB)
        dZ = R["dz"][rows, :]
        acc2 = R["dr2"][rows, :]
        for j in range(gb1.shape[1] // JB):
            js = slice(j * JB, (j + 1) * JB)
            dG = nt(dZ, w2[j].reshape(JB, D))
            dF = (dG * R["df"][rows, js].astype(f32)).astype(bf)
            R["df"][rows, js] = dF
            gb1[:, js] += csum(dF.astype(f32))
            acc2 = acc2 + nt(dF, w1[:, :, :, :, js].reshape(D, JB))
        n1h = R["n1h"][rows, :]
        gv[4:5, :] += csum(acc2 * n1h)
        gv[5:6, :] += csum(acc2)
        dR1 = norm_back(acc2 * vec[8:9, :], n1h, R["mk"][rows, H : H + 1])
        R["n1h"][rows, :] = dR1
        dB = dR1.astype(bf)
        R["db"][rows, :] = dB
        gv[2:3, :] += csum(dB.astype(f32))


def p3_w2(R):
    @pl.loop(0, R["g"].shape[1] // MB)
    def _(j):
        js = pl.ds(pl.multiple_of(j * MB, MB), MB)
        r = tn(R["g"][:, js], R["dz"][...]).astype(bf)
        R["g2"][j // 2, pl.ds((j % 2) * 2, 2)] = r.reshape(2, 2, 64, 512)


def p3_w1(R):
    @pl.loop(0, R["g"].shape[1] // MB)
    def _(j):
        js = pl.ds(pl.multiple_of(j * MB, MB), MB)
        r = tn(R["n1b"][...], R["df"][:, js]).astype(bf)
        R["g1"][:, :, :, :, js] = r.reshape(4, NZ, 2, 16, MB)


def grad_attn(R, i, left, right):
    @pl.loop(0, 512 // MB)
    def _(j):
        js = pl.ds(pl.multiple_of(j * MB, MB), MB)
        r = tn(R[left][:, js], R[right][...]).astype(bf)
        R["ga"][i, pl.ds(j * 2, 2)] = r.reshape(2, NZ, 2, 16, 512)


def spare(R, i):
    return R["g"].at[0:1024, i * 256 : (i + 1) * 256]


def p4(R, hook=nohook, done=nohook):
    gv = R["gv"]
    R["g"][0:1024, :] = jnp.zeros((1024, R["g"].shape[1]), bf)

    @pl.loop(0, R["x"].shape[0] // TM1)
    def _(i):
        hook(i)
        r0 = pl.multiple_of(i * TM1, TM1)
        rows = pl.ds(r0, TM1)
        dC = nt(R["db"][rows, :], wmat(R, 3))
        a = []
        b = []
        d = []
        for s in range(PW):
            rs = pl.ds(pl.multiple_of(r0 + s * L, L), L)
            dq, dk, dv = attn_bwd(
                R["q"][rs, :], R["k"][rs, :], R["v"][rs, :], R["ab"][rs, :], dC[s * L : (s + 1) * L],
                R["mk"][rs, 0:H], R["kbd"].at[s], R["vbd"].at[s], spare(R, 2 * s), spare(R, 2 * s + 1),
            )
            a.append(dq)
            b.append(dk)
            d.append(dv)
        dq = jnp.concatenate(a, 0)
        dk = jnp.concatenate(b, 0)
        dv = jnp.concatenate(d, 0)
        R["q"][rows, :] = dq
        R["k"][rows, :] = dk
        R["v"][rows, :] = dv
        gv[0:1, :] += csum(dq.astype(f32))
        gv[1:2, :] += csum(dv.astype(f32))
        gx = R["n1h"][rows, :] + nt(dq, wmat(R, 0)) + nt(dk, wmat(R, 1)) + nt(dv, wmat(R, 2))
        R["dx"][rows, :] = gx.astype(bf)
        done(i)


def scratch_of(T, D, FFW):
    V = pltpu.VMEM
    return dict(
        kbd=V((PW, 1024, 256), bf), vbd=V((PW, 1024, 256), bf), mk=V((T, 16), f32),
        q=V((T, D), bf), k=V((T, D), bf), v=V((T, D), bf), ab=V((T, 1024), bf), c=V((T, D), bf),
        n1h=V((T, D), f32), n1b=V((T, D), bf), g=V((T, FFW), bf), df=V((T, FFW), bf),
        dz=V((T, D), bf), dr2=V((T, D), f32), b1=V((1, FFW), f32),
    )


def compute(x, cot, idx, vec, wa, w1, w2):
    T, D = x.shape
    FFW = 4 * D
    sc = scratch_of(T, D, FFW)
    ins = ["x", "cot", "idx", "vec", "wa", "w1", "w2"]
    outs = dict(
        y=SDS((T, D), bf), dx=SDS((T, D), bf), ga=SDS(wa.shape, bf), g1=SDS(w1.shape, bf), g2=SDS(w2.shape, bf),
        gv=SDS((8, D), f32), gb1=SDS((1, FFW), f32),
    )
    names = ins + list(outs) + list(sc)

    def kern(*refs):
        R = dict(zip(names, refs))
        R["db"] = R["dz"]
        p0(R, lax.axis_index("chan") * (T // L))
        p1(R)
        p2_inner(R)
        p2_outer(R)
        p3_w2(R)
        p2_back(R)
        p3_w1(R)
        grad_attn(R, 3, "c", "db")
        p4(R)
        for i, n in enumerate(("q", "k", "v")):
            grad_attn(R, i, "x", n)

    vm = pl.BlockSpec(memory_space=pltpu.VMEM)
    return pl.pallas_call(
        kern, out_shape=list(outs.values()), in_specs=[vm] * len(ins), out_specs=[vm] * len(outs),
        scratch_shapes=list(sc.values()), compiler_params=pltpu.CompilerParams(vmem_limit_bytes=63 << 20),
    )(x, cot, idx, vec, wa, w1, w2)


MESH = pl.DeviceIdType.MESH
CH = 192


class Copies:
    def __init__(self, ss, rs):
        self.ss, self.rs, self.n = ss, rs, 0
        self.sent = []

    def ids(self, count):
        first = self.n
        self.n += count
        return first

    def make(self, i, src, dst, peer):
        return pltpu.make_async_remote_copy(
            src_ref=src, dst_ref=dst, send_sem=self.ss.at[i], recv_sem=self.rs.at[i], device_id=peer,
            device_id_type=MESH,
        )


N_SEM = 256
N_LOC = 16


def lamb_update(w, g, m, v):
    m2 = beta_first * m + (1.0 - beta_first) * g
    v2 = beta_second * v + (1.0 - beta_second) * g * g
    r = m2 / (1.0 - beta_first**STEP) / (jnp.sqrt(v2 / (1.0 - beta_second**STEP)) + epsilon) + weight_decay * w
    return m2, v2, r


def row_squares(v):
    return jnp.sum(v * v, axis=1, keepdims=True)


def mega(inputs, cotangent, idx, vec, aw, am, av, fw, fm, fv):
    T = inputs.shape[0] // 4
    D = vec.shape[1]
    FFW = 4 * D
    NC = T // CH
    V = pltpu.VMEM
    ins = ["xin", "cin", "idx", "vec", "aw", "am", "av", "fw", "fm", "fv"]
    outs = dict(
        yo=SDS(inputs.shape, bf), dxo=SDS(inputs.shape, bf), oa=SDS(aw.shape, f32), of=SDS(fw.shape, f32),
        ov=SDS((12, D), f32), sq=SDS((8, 128), f32),
    )
    sc = scratch_of(T, D, FFW)
    sc.update(
        x=V((T, D), bf), cot=V((T, D), bf), wa=V((4, 4, NZ, 2, 16, D), bf), w1=V((4, NZ, 2, 16, FFW), bf),
        w2=V((4, NZ, 2, 64, D), bf), ga=V((4, 4, NZ, 2, 16, D), bf), g1=V((4, NZ, 2, 16, FFW), bf),
        g2=V((4, NZ, 2, 64, D), bf), gv=V((8, D), f32), gb1=V((1, FFW), f32),
        ra0=V((4, 4, NZ, 16, D), bf), r10=V((4, NZ, 16, FFW), bf), r20=V((4, NZ, 64, D), bf),
        rax=V((4, 3, NZ, 16, D), bf), raz=V((4, 3, 16, D), bf),
        r1z=V((3, 4, 16, FFW), bf), r1x=V((3, 16, FFW), bf),
        r2z=V((3, 4, 64, D), bf), r2x=V((3, 64, D), bf),
        va=V((16, D), f32), vb=V((16, D), f32), vx=V((4, 16, D), f32), vz=V((NZ, 16, D), f32),
        sh_a=V((4, 16, D), bf), sh_1=V((16, FFW), bf), sh_2=V((64, D), bf), rows=V((64, FFW), f32),
        qa=V((8, 128), f32), qb=V((8, 128), f32), qx=V((4, 8, 128), f32), qz=V((NZ, 8, 128), f32),
        ss=pltpu.SemaphoreType.DMA((N_SEM,)), rs=pltpu.SemaphoreType.DMA((N_SEM,)),
        ls=pltpu.SemaphoreType.DMA((N_LOC,)),
    )
    names = ins + list(outs) + list(sc)

    def kern(*refs):
        R = dict(zip(names, refs))
        R["y"] = R["cot"]
        R["dx"] = R["c"]
        R["db"] = R["dz"]
        ch = lax.axis_index("chan")
        ro = lax.axis_index("rows")
        z = ro // 2
        c = ro % 2
        o = 1 - c
        px = [(ch ^ d, ro) for d in (1, 2, 3)]
        pz = [(ch, (z ^ d) * 2 + c) for d in (1, 2, 3)]
        pc = (ch, z * 2 + o)
        middle = jnp.logical_or(z == 1, z == 2)
        C = Copies(R["ss"], R["rs"])
        ls = R["ls"]

        def rows_in(src, dst, first):
            def cp(k, d):
                return C.make(
                    first + k * 3 + d - 1, src.at[pl.ds((ch ^ d) * T + k * CH, CH), :],
                    dst.at[pl.ds(k * CH, CH), pl.ds(pl.multiple_of(ch * 128, 128), 128)], px[d - 1],
                )
            return cp

        def rows_out(src, dst, first):
            def cp(k, d):
                return C.make(
                    first + k * 3 + d - 1,
                    src.at[pl.ds(k * CH, CH), pl.ds(pl.multiple_of((ch ^ d) * 128, 128), 128)],
                    dst.at[pl.ds(ch * T + k * CH, CH), :], px[d - 1],
                )
            return cp

        x_cp = rows_in(R["xin"], R["x"], C.ids(3 * NC))
        c_cp = rows_in(R["cin"], R["cot"], C.ids(3 * NC))
        y_cp = rows_out(R["y"], R["yo"], C.ids(3 * NC))
        dx_cp = rows_out(R["dx"], R["dxo"], C.ids(3 * NC))
        DS = (1, 2, 3)
        own = pl.ds(pl.multiple_of(ch * 128, 128), 128)
        x_loc = pltpu.make_async_copy(R["xin"].at[pl.ds(ch * T, T), :], R["x"].at[:, own], ls.at[0])
        c_loc = pltpu.make_async_copy(R["cin"].at[pl.ds(ch * T, T), :], R["cot"].at[:, own], ls.at[1])
        y_loc = pltpu.make_async_copy(R["y"].at[:, own], R["yo"].at[pl.ds(ch * T, T), :], ls.at[2])
        dx_loc = pltpu.make_async_copy(R["dx"].at[:, own], R["dxo"].at[pl.ds(ch * T, T), :], ls.at[3])

        class Gather:
            def __init__(self, shard, loc, place, sets):
                ia, ib, ic, iw = C.ids(3), C.ids(3), C.ids(4), C.ids(1)
                self.loc = pltpu.make_async_copy(shard, place(ch, z, c), ls.at[loc])
                self.plane = [C.make(ia + d - 1, shard, place(ch, z, c), px[d - 1]) for d in DS]
                self.chain = [C.make(ib + d - 1, sets(z, c), sets(z, c), pz[d - 1]) for d in DS]
                self.onward = pltpu.make_async_remote_copy(
                    src_ref=sets(z ^ 2, c), dst_ref=sets(z ^ 2, c), send_sem=C.ss.at[iw], recv_sem=C.rs.at[ib + 2],
                    device_id=pz[0], device_id_type=MESH,
                )
                self.core = [C.make(ic + d, sets(z ^ d, c), sets(z ^ d, c), pc) for d in range(4)]

            def start(self):
                for cp in self.plane:
                    cp.start()
                self.loc.start()

            def along(self):
                self.loc.wait()
                for cp in self.plane:
                    cp.wait_recv()
                for cp in self.chain[:2]:
                    cp.start()

                @pl.when(middle)
                def _():
                    self.chain[2].start()

                self.core[0].start()

            def near(self):
                self.chain[0].wait_recv()
                self.core[1].start()
                self.chain[1].wait_recv()

                @pl.when(middle)
                def _():
                    self.onward.start()

                self.core[2].start()

            def far(self):
                self.chain[2].wait_recv()
                self.core[3].start()

            def arrive(self):
                for cp in self.core:
                    cp.wait_recv()

            def finish(self):
                for cp in self.plane + self.chain[:2] + self.core:
                    cp.wait_send()

                @pl.when(middle)
                def _():
                    self.chain[2].wait_send()
                    self.onward.wait_send()

        class GatherZ:
            def __init__(self, shard, loc, place, sets):
                ia, ib, ic = C.ids(3), C.ids(12), C.ids(4)
                self.loc = pltpu.make_async_copy(shard, place(ch, z, c), ls.at[loc])
                self.chain = [C.make(ia + d - 1, shard, place(ch, z, c), pz[d - 1]) for d in DS]
                self.plane = [
                    [
                        C.make(ib + e * 3 + d - 1, place(ch, z ^ e, c) if e else shard, place(ch, z ^ e, c), px[d - 1])
                        for d in DS
                    ]
                    for e in range(4)
                ]
                self.core = [C.make(ic + d, sets(ch ^ d, c), sets(ch ^ d, c), pc) for d in range(4)]

            def start(self):
                for cp in self.chain + self.plane[0]:
                    cp.start()
                self.loc.start()

            def along(self):
                for e in DS:
                    self.chain[e - 1].wait_recv()
                    for cp in self.plane[e]:
                        cp.start()
                self.loc.wait()
                self.core[0].start()

            def near(self):
                for d in DS:
                    for e in range(4):
                        self.plane[e][d - 1].wait_recv()
                    self.core[d].start()

            def arrive(self):
                for cp in self.core:
                    cp.wait_recv()

            def finish(self):
                for cp in sum(self.plane, []) + self.chain + self.core:
                    cp.wait_send()

        wa, w1, w2 = R["wa"], R["w1"], R["w2"]
        A2, LO, HI = pl.ds(0, 2), pl.ds(0, 32), pl.ds(32, 32)
        sa, s1, s2 = R["sh_a"], R["sh_1"], R["sh_2"]
        GA = GatherZ(sa.at[A2], 4, lambda a, b, e: wa.at[A2, a, b, e], lambda a, e: wa.at[A2, a, :, e])
        GV = Gather(sa.at[2], 9, lambda a, b, e: wa.at[2, a, b, e], lambda b, e: wa.at[2, :, b, e])
        GO = Gather(sa.at[3], 5, lambda a, b, e: wa.at[3, a, b, e], lambda b, e: wa.at[3, :, b, e])
        G1 = Gather(s1, 6, lambda a, b, e: w1.at[a, b, e], lambda b, e: w1.at[:, b, e])
        G2 = Gather(s2.at[LO], 7, lambda a, b, e: w2.at[a, b, e, LO], lambda b, e: w2.at[:, b, e, LO])
        G3 = GatherZ(s2.at[HI], 8, lambda a, b, e: w2.at[a, b, e, HI], lambda a, e: w2.at[a, :, e, HI])

        class Scatter:
            def __init__(self, g, out, b0, bx, bz, plane_first):
                i0, i1, i2 = C.ids(1), C.ids(3), C.ids(3)
                self.g, self.out, self.b0, self.bx, self.bz, self.plane_first = g, out, b0, bx, bz, plane_first
                self.s0 = C.make(i0, g.at[:, :, o], b0, pc)
                if plane_first:
                    self.s1 = [C.make(i1 + d - 1, g.at[ch ^ d, :, c], bx.at[d - 1], px[d - 1]) for d in DS]
                    self.s2 = [C.make(i2 + d - 1, g.at[ch, z ^ d, c], bz.at[d - 1], pz[d - 1]) for d in DS]
                else:
                    self.s1 = [C.make(i1 + d - 1, g.at[:, z ^ d, c], bz.at[d - 1], pz[d - 1]) for d in DS]
                    self.s2 = [C.make(i2 + d - 1, g.at[ch ^ d, z, c], bx.at[d - 1], px[d - 1]) for d in DS]

            def begin(self):
                self.s0.start()

            def one(self):
                self.s0.wait_recv()
                g = self.g

                @pl.loop(0, 4)
                def _(j):
                    g[j, :, c] = (g[j, :, c].astype(f32) + self.b0[j].astype(f32)).astype(bf)

                for cp in self.s1:
                    cp.start()

            def two(self):
                for cp in self.s1:
                    cp.wait_recv()
                g = self.g
                b = self.bx if self.plane_first else self.bz

                @pl.loop(0, 4)
                def _(j):
                    t = b[0, j].astype(f32) + b[1, j].astype(f32) + b[2, j].astype(f32)
                    if self.plane_first:
                        g[ch, j, c] = (g[ch, j, c].astype(f32) + t).astype(bf)
                    else:
                        g[j, z, c] = (g[j, z, c].astype(f32) + t).astype(bf)

                for cp in self.s2:
                    cp.start()

            def three(self):
                for cp in self.s2:
                    cp.wait_recv()
                b = self.bz if self.plane_first else self.bx
                t = b[0].astype(f32) + b[1].astype(f32) + b[2].astype(f32)
                t = self.g[ch, z, c].astype(f32) + t
                ref, row = self.out
                n = t.shape[1]
                for k in range(t.shape[0]):
                    ref[row : row + 1, k * n : (k + 1) * n] = t[k : k + 1, :]

            def finish(self):
                for cp in [self.s0] + self.s1 + self.s2:
                    cp.wait_send()

        S1 = Scatter(R["g1"], (R["of"], 0), R["r10"], R["r1x"], R["r1z"], False)
        S2 = Scatter(R["g2"], (R["of"], 1), R["r20"], R["r2x"], R["r2z"], False)
        SA = [Scatter(R["ga"].at[0], (R["oa"], 0), R["ra0"].at[0], R["raz"].at[0], R["rax"].at[0], False)] + [
            Scatter(R["ga"].at[i], (R["oa"], i), R["ra0"].at[i], R["rax"].at[i], R["raz"].at[i], True) for i in (1, 2, 3)
        ]
        va, vb, vx, vz = R["va"], R["vb"], R["vx"], R["vz"]
        iv = C.ids(7)
        v0 = C.make(iv, va, vb, pc)
        v1 = [C.make(iv + d, vx.at[ch], vx.at[ch], px[d - 1]) for d in DS]
        v2 = [C.make(iv + 3 + d, vz.at[z], vz.at[z], pz[d - 1]) for d in DS]
        qa, qb, qx, qz = R["qa"], R["qb"], R["qx"], R["qz"]
        iq = C.ids(7)
        q0 = C.make(iq, qa, qb, pc)
        q1 = [C.make(iq + d, qx.at[ch], qx.at[ch], px[d - 1]) for d in DS]
        q2 = [C.make(iq + 3 + d, qz.at[z], qz.at[z], pz[d - 1]) for d in DS]
        assert C.n <= N_SEM

        bar = pltpu.get_barrier_semaphore()
        for peer in px + pz + [pc]:
            pl.semaphore_signal(bar, inc=1, device_id=peer, device_id_type=MESH)
        x_loc.start()
        c_loc.start()
        tmp = R["rows"]

        def split(src, row, count, n):
            for k in range(count):
                tmp[k : k + 1, 0:n] = src[row : row + 1, k * n : (k + 1) * n]
            return tmp[0:count, 0:n].astype(bf)

        for i in range(4):
            R["sh_a"][i] = split(R["aw"], i, 16, D)
        R["sh_1"][...] = split(R["fw"], 0, 16, FFW)
        R["sh_2"][...] = split(R["fw"], 1, 64, D)
        pl.semaphore_wait(bar, 7)

        GA.start()
        GV.start()
        for d in DS:
            x_cp(0, d).start()
        GO.start()
        G1.start()
        GV.along()
        GA.along()
        G3.start()
        G2.start()

        @pl.loop(1, NC)
        def _(k):
            for d in DS:
                x_cp(k, d).start()

        GO.along()
        G1.along()
        G2.along()
        G3.along()
        p0(R, ch * (T // L))
        GV.near()
        GA.near()
        GO.near()
        GV.far()
        GO.far()
        GA.arrive()
        GV.arrive()
        GO.arrive()
        x_loc.wait()

        def hook1(i):
            for k in range(TM1 // CH):
                for d in DS:
                    x_cp(i * (TM1 // CH) + k, d).wait_recv()
                for d in DS:
                    c_cp(i * (TM1 // CH) + k, d).start()

            @pl.when(i == 2)
            def _():
                G1.near()

            @pl.when(i == 3)
            def _():
                G1.far()

        p1(R, hook1)
        G1.arrive()
        G3.near()
        G2.near()
        p2_inner(R)
        G2.far()
        c_loc.wait()
        G3.arrive()
        G2.arrive()

        def hook2(i):
            for k in range(TM2 // CH):
                for d in DS:
                    c_cp(i * (TM2 // CH) + k, d).wait_recv()

        def done2(i):
            for k in range(TM2 // CH):
                for d in DS:
                    y_cp(i * (TM2 // CH) + k, d).start()

        p2_outer(R, hook2, done2)
        y_loc.start()
        p3_w2(R)
        S2.begin()

        def hook3(i):
            @pl.when(i == 1)
            def _():
                S2.one()

        p2_back(R, hook3)
        p3_w1(R)
        S1.begin()
        grad_attn(R, 3, "c", "db")
        S1.one()
        SA[3].begin()

        def hook4(i):
            @pl.when(i == 1)
            def _():
                SA[3].one()

            @pl.when(i == 2)
            def _():
                S2.two()

        def done4(i):
            for k in range(TM1 // CH):
                for d in DS:
                    dx_cp(i * (TM1 // CH) + k, d).start()

        p4(R, hook4, done4)
        dx_loc.start()
        va[4:12, :] = R["gv"][...]
        for j in range(4):
            va[j : j + 1, :] = R["gb1"][:, j * D : (j + 1) * D]
        va[12:16, :] = jnp.zeros((4, D), f32)
        v0.start()
        grad_attn(R, 0, "x", "q")
        SA[0].begin()
        v0.wait_recv()
        vx[ch] = va[...] + vb[...]
        for cp in v1:
            cp.start()
        grad_attn(R, 1, "x", "k")
        SA[1].begin()
        SA[0].one()
        grad_attn(R, 2, "x", "v")
        SA[2].begin()
        SA[1].one()
        SA[3].two()
        SA[2].one()
        S2.three()
        S1.two()
        for cp in v1:
            cp.wait_recv()
        vz[z] = vx[0] + vx[1] + vx[2] + vx[3]
        for cp in v2:
            cp.start()
        SA[3].three()
        SA[0].two()
        SA[1].two()
        SA[2].two()
        S1.three()
        qa[...] = jnp.zeros_like(qa)
        qa[0:4, 0:1] = row_squares(R["aw"][...])
        qa[4:6, 0:1] = row_squares(R["fw"][...])
        qa[4:6, 1:2] = row_squares(lamb_update(R["fw"][...], R["of"][...], R["fm"][...], R["fv"][...])[2])
        for cp in v2:
            cp.wait_recv()
        tot = vz[0] + vz[1] + vz[2] + vz[3]
        R["ov"][...] = tot[0:12, :]
        for i in range(3):
            SA[i].three()
        qa[0:4, 1:2] = row_squares(lamb_update(R["aw"][...], R["oa"][...], R["am"][...], R["av"][...])[2])
        q0.start()
        q0.wait_recv()
        qx[ch] = qa[...] + qb[...]
        for cp in q1:
            cp.start()
        for cp in q1:
            cp.wait_recv()
        qz[z] = qx[0] + qx[1] + qx[2] + qx[3]
        for cp in q2:
            cp.start()

        @pl.loop(0, NC)
        def _(k):
            for d in DS:
                y_cp(k, d).wait_recv()
                dx_cp(k, d).wait_recv()
                x_cp(k, d).wait_send()
                c_cp(k, d).wait_send()
                y_cp(k, d).wait_send()
                dx_cp(k, d).wait_send()

        y_loc.wait()
        dx_loc.wait()
        for t in (GA, GV, GO, G1, G2, G3, S1, S2, *SA):
            t.finish()
        for cp in q2:
            cp.wait_recv()
        R["sq"][...] = qz[0] + qz[1] + qz[2] + qz[3]
        for cp in [v0, q0] + v1 + v2 + q1 + q2:
            cp.wait_send()

    vm = pl.BlockSpec(memory_space=pltpu.VMEM)
    an = pl.BlockSpec(memory_space=pl.ANY)
    return pl.pallas_call(
        kern, out_shape=list(outs.values()), in_specs=[an, an] + [vm] * 8,
        out_specs=[an, an, vm, vm, vm, vm], scratch_shapes=list(sc.values()),
        compiler_params=pltpu.CompilerParams(
            vmem_limit_bytes=63 << 20, collective_id=0, has_side_effects=True
        ),
    )(inputs, cotangent, idx, vec, aw, am, av, fw, fm, fv)


def finish(yi, dxi, sets, squares):
    shapes = [SDS(yi.shape, bf), SDS(dxi.shape, bf)]
    flat = []
    for w, g, m, v in sets:
        flat += [w, g, m, v]
        shapes += [SDS(w.shape, f32)] * 4
    shapes += [SDS(sets[0][0].shape, bf), SDS(sets[1][0].shape, bf), SDS((2, 6), f32)]
    n = len(flat)

    def kern(*refs):
        ya, xa, sq = refs[0], refs[1], refs[2]
        src = refs[3 : 3 + n]
        yb, xb = refs[3 + n : 5 + n]
        dst = refs[5 + n : 5 + 2 * n]
        low_a, low_f, norms, hold, sems = refs[5 + 2 * n :]
        part = ya.shape[0] // 4
        load = []
        save = []
        for k in range(8):
            rows = pl.ds((k % 4) * part, part)
            src_ref, dst_ref = ((ya, yb), (xa, xb))[k // 4]
            load.append(pltpu.make_async_copy(src_ref.at[rows], hold.at[k], sems.at[k]))
            save.append(pltpu.make_async_copy(hold.at[k], dst_ref.at[rows], sems.at[8 + k]))
        for cp in load:
            cp.start()
        root = jnp.sqrt(sq[...])
        norms[...] = jnp.transpose(root)[0:2, 0:6]
        for k in range(8):
            load[k].wait()
            save[k].start()
        ratio = root[:, 0:1] * lax.rsqrt(sq[:, 1:2] + epsilon)
        for k in range(3):
            w, g, m, v = [r[...] for r in src[4 * k : 4 * k + 4]]
            m2, v2, r = lamb_update(w, g, m, v)
            if k == 2:
                rate = jnp.sqrt(row_squares(w)) * lax.rsqrt(row_squares(r) + epsilon)
            else:
                rate = ratio[0:4] if k == 0 else ratio[4:6]
            new = w - learn_rate * rate * r
            for ref, val in zip(dst[4 * k : 4 * k + 4], (new, g, m2, v2)):
                ref[...] = val
            if k < 2:
                (low_a, low_f)[k][...] = new.astype(bf)
        for cp in save:
            cp.wait()

    vm = pl.BlockSpec(memory_space=pltpu.VMEM)
    an = pl.BlockSpec(memory_space=pl.ANY)
    return pl.pallas_call(
        kern, out_shape=shapes, in_specs=[an, an] + [vm] * (1 + n), out_specs=[an, an] + [vm] * (n + 3),
        scratch_shapes=[
            pltpu.VMEM((8, yi.shape[0] // 4, yi.shape[1]), bf), pltpu.SemaphoreType.DMA((16,)),
        ],
        compiler_params=pltpu.CompilerParams(vmem_limit_bytes=63 << 20),
    )(yi, dxi, squares, *flat)


def native(inputs, cotangent, idx, vec, aw, am, av, fw, fm, fv):
    axes = ("chan", "rows")
    D = vec.shape[1]
    x = lax.all_to_all(inputs, "chan", split_axis=0, concat_axis=1, tiled=True)
    cot = lax.all_to_all(cotangent, "chan", split_axis=0, concat_axis=1, tiled=True)
    wa = lax.all_gather(aw.astype(bf), axes, axis=1, tiled=True)
    wf = lax.all_gather(fw.astype(bf), axes, axis=1, tiled=True)
    y, dx, ga, g1, g2, gv, gb1 = compute(
        x, cot, idx, vec, wa.reshape(4, 4, NZ, 2, 16, D), wf[0].reshape(4, NZ, 2, 16, -1), wf[1].reshape(4, NZ, 2, 64, D)
    )
    yo = lax.all_to_all(y, "chan", split_axis=1, concat_axis=0, tiled=True)
    dxo = lax.all_to_all(dx, "chan", split_axis=1, concat_axis=0, tiled=True)
    ga = ga.reshape(4, -1).astype(f32)
    gf = jnp.stack([g1.reshape(-1), g2.reshape(-1)]).astype(f32)
    ga = lax.psum_scatter(ga, axes, scatter_dimension=1, tiled=True)
    gf = lax.psum_scatter(gf, axes, scatter_dimension=1, tiled=True)
    gv = lax.psum(jnp.concatenate([gb1.reshape(4, D), gv], axis=0), axes)
    part = []
    for w, g, m, v in ((aw, ga, am, av), (fw, gf, fm, fv)):
        part.append(jnp.concatenate([row_squares(w), row_squares(lamb_update(w, g, m, v)[2])], axis=1))
    squares = jnp.zeros((8, 128), f32).at[0:6, 0:2].set(lax.psum(jnp.concatenate(part, axis=0), axes))
    return yo, dxo, ga, gf, gv, squares


def step(move, inputs, cotangent, top_index, aw, am, av, fw, fm, fv, vec, vm, vv):
    yo, dxo, ga, gf, gv, squares = move(inputs, cotangent, jnp.transpose(top_index, (2, 1, 0)), vec, aw, am, av, fw, fm, fv)
    sets = ((aw, ga, am, av), (fw, gf, fm, fv), (vec, gv, vm, vv))
    r = finish(yo, dxo, sets, squares)
    aw2, ga, am2, av2, fw2, gf, fm2, fv2, vec2, gv, vm2, vv2 = r[2:14]
    return r[0], r[1], ga, gf, gv, am2, av2, fm2, fv2, vm2, vv2, aw2, fw2, vec2, r[14], r[15], r[16].T


def solution(mesh):
    small = mesh.shape["chan"] == 4 and mesh.shape["rows"] == 2 * NZ
    local = functools.partial(step, mega if small else native)
    in_specs = (
        P("rows", "chan"),
        P("rows", "chan"),
        P("rows", None, None),
        P(None, ("chan", "rows")),
        P(None, ("chan", "rows")),
        P(None, ("chan", "rows")),
        P(None, ("chan", "rows")),
        P(None, ("chan", "rows")),
        P(None, ("chan", "rows")),
        P(),
        P(),
        P(),
    )
    out_specs = (
        P("rows", "chan"),
        P("rows", "chan"),
        P(None, ("chan", "rows")),
        P(None, ("chan", "rows")),
        P(),
        P(None, ("chan", "rows")),
        P(None, ("chan", "rows")),
        P(None, ("chan", "rows")),
        P(None, ("chan", "rows")),
        P(),
        P(),
        P(None, ("chan", "rows")),
        P(None, ("chan", "rows")),
        P(),
        P(None, ("chan", "rows")),
        P(None, ("chan", "rows")),
        P(),
    )
    return jax.shard_map(local, mesh=mesh, in_specs=in_specs, out_specs=out_specs, check_vma=False)
```

```python
import functools

import jax
import jax.numpy as jnp
from jax import lax
from jax.experimental import pallas as pl
from jax.experimental.pallas import tpu as pltpu
from jax.sharding import PartitionSpec as P

STEP = 3
epsilon = 1e-06
beta_first = 0.5
beta_second = 0.5
learn_rate = 0.3
weight_decay = 0.01


bf = jnp.bfloat16
f32 = jnp.float32
L = 96
H = 8
NZ = 4
SC = 0.125
EPS = 1e-5
SDS = jax.ShapeDtypeStruct


def _dg(a, b, ca, cb):
    return lax.dot_general(a, b, (((ca,), (cb,)), ((), ())), preferred_element_type=f32)


def nn(a, b):
    return _dg(a, b, 1, 0)


def nt(a, b):
    return _dg(a, b, 1, 1)


def tn(a, b):
    return _dg(a, b, 0, 0)


def csum(v):
    return jnp.sum(v, axis=0, keepdims=True)


def gelu_both(F):
    ph = 0.5 * (1.0 + lax.erf(F * 0.7071067811865476))
    pdf = jnp.exp(-0.5 * F * F) * 0.3989422804014327
    return F * ph, ph + F * pdf


def norm_parts(r):
    cen = r - jnp.mean(r, axis=-1, keepdims=True)
    var = jnp.mean(cen * cen, axis=-1, keepdims=True)
    rs = lax.rsqrt(var + EPS)
    return cen * rs, rs


def norm_back(gh, n, rs):
    return rs * (gh - jnp.mean(gh, axis=-1, keepdims=True) - n * jnp.mean(gh * n, axis=-1, keepdims=True))


def pick_mask(idx, lane, w, mk_ref):
    n = idx.shape[1]
    one = (lax.broadcasted_iota(jnp.int32, (n, 128), 0) == lane).astype(bf)
    pos = nn(idx, one)
    li = lax.broadcasted_iota(jnp.int32, (H, 128), 1).astype(f32)
    m = jnp.zeros((H, 128), f32)
    for j in range(idx.shape[0] // H):
        m = jnp.where(li == pos[j * H : (j + 1) * H, :], 1.0, m)
    mk_ref[pl.ds(pl.multiple_of(w * L, L), L), 0:H] = jnp.transpose(m)[0:L, :]


def fill_bd(bd, val):
    li = lax.broadcasted_iota(jnp.int32, (L, 128), 1)
    z = jnp.zeros((L, 128), bf)
    for h in range(H):
        p = h // 2
        blk = jnp.where((li < 64) if h % 2 == 0 else (li >= 64), val[:, p * 128 : (p + 1) * 128], z)
        bd[h * 128 : h * 128 + L, (p % 2) * 128 : (p % 2) * 128 + 128] = blk


def attn_fwd(q, k, v, m8, kbd, vbd, ab_ref, r0):
    fill_bd(kbd, k)
    fill_bd(vbd, v)
    li = lax.broadcasted_iota(jnp.int32, (L, 128), 1)
    mean = csum(v.astype(f32)) * (1.0 / L)
    outs = []
    for g in range(2):
        S = nt(q[:, g * 256 : (g + 1) * 256], kbd[g * 512 : (g + 1) * 512, :])
        abs_ = []
        mb = []
        for hh in range(4):
            h = g * 4 + hh
            mh = jnp.broadcast_to(m8[:, h : h + 1], (L, 128))
            mb.append(mh)
            picked = mh > 0.5
            sh = jnp.where(picked, S[:, hh * 128 : (hh + 1) * 128] * SC, 0.0)
            e = jnp.where(li < L, jnp.exp(sh), 0.0)
            r = jnp.sum(e, axis=1, keepdims=True)
            abs_.append(jnp.where(picked, e * (1.0 / r), 0.0).astype(bf))
        ab = jnp.concatenate(abs_, axis=1)
        ab_ref[pl.ds(r0, L), g * 512 : (g + 1) * 512] = ab
        O = nn(ab, vbd[g * 512 : (g + 1) * 512, :])
        for pp in range(2):
            msk = jnp.where(li < 64, mb[2 * pp], mb[2 * pp + 1]) > 0.5
            c0 = g * 256 + pp * 128
            outs.append(jnp.where(msk, O[:, pp * 128 : (pp + 1) * 128], mean[:, c0 : c0 + 128]))
    return jnp.concatenate(outs, axis=1).astype(bf)


def heads_down(blocks):
    z = jnp.zeros((128 - L, 128), bf)
    return jnp.concatenate([jnp.transpose(jnp.concatenate([b, z], 0))[0:L] for b in blocks], axis=1)


def attn_bwd(q, k, v, ab, dC, m8, kbd, vbd, qbd, obd):
    fill_bd(kbd, k)
    fill_bd(vbd, v)
    fill_bd(qbd, q)
    li = lax.broadcasted_iota(jnp.int32, (L, 128), 1)
    msks = []
    for p in range(4):
        mlo = jnp.broadcast_to(m8[:, 2 * p : 2 * p + 1], (L, 128))
        mhi = jnp.broadcast_to(m8[:, 2 * p + 1 : 2 * p + 2], (L, 128))
        msks.append(jnp.where(li < 64, mlo, mhi))
    msk = jnp.concatenate(msks, axis=1) > 0.5
    dO = jnp.where(msk, dC, 0.0).astype(bf)
    fill_bd(obd, dO)
    dM = csum(jnp.where(msk, 0.0, dC)) * (1.0 / L)
    dqs = []
    dks = []
    dvs = []
    for g in range(2):
        c = slice(g * 256, (g + 1) * 256)
        dA = nt(dO[:, c], vbd[g * 512 : (g + 1) * 512, :])
        dss = []
        for hh in range(4):
            h = g * 4 + hh
            a = ab[:, h * 128 : (h + 1) * 128].astype(f32)
            t = a * dA[:, hh * 128 : (hh + 1) * 128]
            r = jnp.sum(t, axis=1, keepdims=True)
            dss.append((t - a * r).astype(bf))
        dS = jnp.concatenate(dss, axis=1)
        dqs.append(nn(dS, kbd[g * 512 : (g + 1) * 512, :]) * SC)
        half = slice(g * 512, (g + 1) * 512)
        dks.append(nn(heads_down(dss), qbd[half, :]) * SC)
        dvs.append(nn(heads_down([ab[:, h * 128 : (h + 1) * 128] for h in range(g * 4, g * 4 + 4)]), obd[half, :]))
    dQ = jnp.concatenate(dqs, axis=1).astype(bf)
    dK = jnp.concatenate(dks, axis=1).astype(bf)
    dV = (jnp.concatenate(dvs, axis=1) + dM).astype(bf)
    return dQ, dK, dV


def wmat(R, i):
    v = R["wa"][i]
    return v.reshape(512, 512)


def nohook(i):
    pass


PW = 4
TM1 = PW * L
TMF = 512
TM2 = 384
TMB = 512
JB = 512
MB = 256


def p0(R, first):
    R["kbd"][...] = jnp.zeros_like(R["kbd"])
    R["vbd"][...] = jnp.zeros_like(R["vbd"])
    R["gv"][...] = jnp.zeros_like(R["gv"])
    R["gb1"][...] = jnp.zeros_like(R["gb1"])
    D = R["vec"].shape[1]
    for j in range(4):
        R["b1"][:, j * D : (j + 1) * D] = R["vec"][j : j + 1, :]

    n = R["idx"].shape
    R["ib"][...] = R["idx"][...].astype(f32).reshape(n[0] * n[1], n[2]).astype(bf)

    @pl.loop(0, R["x"].shape[0] // (4 * L))
    def _(w):
        for u in range(4):
            pick_mask(R["ib"][...], first + w * 4 + u, w * 4 + u, R["mk"])


def p1(R, hook=nohook, late=nohook):
    x, vec = R["x"], R["vec"]

    @pl.loop(0, x.shape[0] // TM1)
    def _(i):
        hook(i)
        r0 = pl.multiple_of(i * TM1, TM1)
        rows = pl.ds(r0, TM1)
        xb = x[rows, :]
        q = (nn(xb, wmat(R, 0)) + vec[4:5, :]).astype(bf)
        k = nn(xb, wmat(R, 1)).astype(bf)
        v = (nn(xb, wmat(R, 2)) + vec[5:6, :]).astype(bf)
        R["q"][rows, :] = q
        R["k"][rows, :] = k
        R["v"][rows, :] = v
        cs = []
        for s in range(PW):
            sl = slice(s * L, (s + 1) * L)
            r1 = pl.multiple_of(r0 + s * L, L)
            cs.append(
                attn_fwd(
                    q[sl], k[sl], v[sl], R["mk"][pl.ds(r1, L), 0:H], R["kbd"].at[s], R["vbd"].at[s], R["ab"], r1
                )
            )
        c = jnp.concatenate(cs, axis=0)
        R["c"][rows, :] = c
        late(i)
        n, rs = norm_parts(xb.astype(f32) + (nn(c, wmat(R, 3)) + vec[6:7, :]))
        R["n1h"][rows, :] = n
        R["mk"][rows, H : H + 1] = rs
        R["n1b"][rows, :] = (n * vec[8:9, :] + vec[9:10, :]).astype(bf)


def p2_inner(R, hook=nohook):
    w1, b1 = R["w1"], R["b1"]
    D = R["vec"].shape[1]

    @pl.loop(0, R["x"].shape[0] // TMF)
    def _(i):
        hook(i)
        rows = pl.ds(pl.multiple_of(i * TMF, TMF), TMF)
        n1b = R["n1b"][rows, :]
        for j in range(b1.shape[1] // JB):
            js = slice(j * JB, (j + 1) * JB)
            G, sl = gelu_both(nn(n1b, w1[:, :, :, :, js].reshape(D, JB)) + b1[:, js])
            R["g"][rows, js] = G.astype(bf)
            R["df"][rows, js] = sl.astype(bf)


def p2_outer(R, hook=nohook, done=nohook):
    vec, w2, cot, gv = R["vec"], R["w2"], R["cot"], R["gv"]
    D = vec.shape[1]
    FFW = R["b1"].shape[1]

    @pl.loop(0, cot.shape[0] // TM2)
    def _(i):
        hook(i)
        rows = pl.ds(pl.multiple_of(i * TM2, TM2), TM2)
        acc = R["n1h"][rows, :] * vec[8:9, :] + vec[9:10, :] + vec[7:8, :]
        acc = acc + nn(R["g"][rows, :], w2[...].reshape(FFW, D))
        yh, rs2 = norm_parts(acc)
        dY = cot[rows, :].astype(f32)
        R["y"][rows, :] = (yh * vec[10:11, :] + vec[11:12, :]).astype(bf)
        done(i)
        gv[6:7, :] += csum(dY * yh)
        gv[7:8, :] += csum(dY)
        dR2 = norm_back(dY * vec[10:11, :], yh, rs2)
        R["dr2"][rows, :] = dR2
        dZ = dR2.astype(bf)
        R["dz"][rows, :] = dZ
        gv[3:4, :] += csum(dZ.astype(f32))


def p2_back(R, hook=nohook):
    vec, w1, w2, gv, gb1 = R["vec"], R["w1"], R["w2"], R["gv"], R["gb1"]
    D = vec.shape[1]

    @pl.loop(0, R["x"].shape[0] // TMB)
    def _(i):
        hook(i)
        rows = pl.ds(pl.multiple_of(i * TMB, TMB), TMB)
        dZ = R["dz"][rows, :]
        acc2 = R["dr2"][rows, :]
        for j in range(gb1.shape[1] // JB):
            js = slice(j * JB, (j + 1) * JB)
            dG = nt(dZ, w2[j].reshape(JB, D))
            dF = (dG * R["df"][rows, js].astype(f32)).astype(bf)
            R["df"][rows, js] = dF
            gb1[:, js] += csum(dF.astype(f32))
            acc2 = acc2 + nt(dF, w1[:, :, :, :, js].reshape(D, JB))
        n1h = R["n1h"][rows, :]
        gv[4:5, :] += csum(acc2 * n1h)
        gv[5:6, :] += csum(acc2)
        dR1 = norm_back(acc2 * vec[8:9, :], n1h, R["mk"][rows, H : H + 1])
        R["n1h"][rows, :] = dR1
        dB = dR1.astype(bf)
        R["db"][rows, :] = dB
        gv[2:3, :] += csum(dB.astype(f32))


def p3_w2(R):
    @pl.loop(0, R["g"].shape[1] // MB)
    def _(j):
        js = pl.ds(pl.multiple_of(j * MB, MB), MB)
        r = tn(R["g"][:, js], R["dz"][...]).astype(bf)
        R["g2"][j // 2, pl.ds((j % 2) * 2, 2)] = r.reshape(2, 2, 64, 512)


def p3_w1(R):
    @pl.loop(0, R["g"].shape[1] // MB)
    def _(j):
        js = pl.ds(pl.multiple_of(j * MB, MB), MB)
        r = tn(R["n1b"][...], R["df"][:, js]).astype(bf)
        R["g1"][:, :, :, :, js] = r.reshape(4, NZ, 2, 16, MB)


def grad_attn(R, i, left, right):
    @pl.loop(0, 512 // MB)
    def _(j):
        js = pl.ds(pl.multiple_of(j * MB, MB), MB)
        r = tn(R[left][:, js], R[right][...]).astype(bf)
        R["ga"][i, pl.ds(j * 2, 2)] = r.reshape(2, NZ, 2, 16, 512)


def spare(R, i):
    return R["g"].at[0:1024, i * 256 : (i + 1) * 256]


def p4(R, hook=nohook, done=nohook):
    gv = R["gv"]
    for h in range(H):
        R["g"][h * 128 + L : (h + 1) * 128, :] = jnp.zeros((128 - L, R["g"].shape[1]), bf)
        for i in range(2 * PW):
            c0 = i * 256 + 128 * (1 - (h // 2) % 2)
            R["g"][h * 128 : h * 128 + L, c0 : c0 + 128] = jnp.zeros((L, 128), bf)

    @pl.loop(0, R["x"].shape[0] // TM1)
    def _(i):
        hook(i)
        r0 = pl.multiple_of(i * TM1, TM1)
        rows = pl.ds(r0, TM1)
        dC = nt(R["db"][rows, :], wmat(R, 3))
        a = []
        b = []
        d = []
        for s in range(PW):
            rs = pl.ds(pl.multiple_of(r0 + s * L, L), L)
            dq, dk, dv = attn_bwd(
                R["q"][rs, :], R["k"][rs, :], R["v"][rs, :], R["ab"][rs, :], dC[s * L : (s + 1) * L],
                R["mk"][rs, 0:H], R["kbd"].at[s], R["vbd"].at[s], spare(R, 2 * s), spare(R, 2 * s + 1),
            )
            a.append(dq)
            b.append(dk)
            d.append(dv)
        dq = jnp.concatenate(a, 0)
        dk = jnp.concatenate(b, 0)
        dv = jnp.concatenate(d, 0)
        R["q"][rows, :] = dq
        R["k"][rows, :] = dk
        R["v"][rows, :] = dv
        gv[0:1, :] += csum(dq.astype(f32))
        gv[1:2, :] += csum(dv.astype(f32))
        gx = R["n1h"][rows, :] + nt(dq, wmat(R, 0)) + nt(dk, wmat(R, 1)) + nt(dv, wmat(R, 2))
        R["dx"][rows, :] = gx.astype(bf)
        done(i)


def scratch_of(T, D, FFW, picks):
    V = pltpu.VMEM
    return dict(
        kbd=V((PW, 1024, 256), bf), vbd=V((PW, 1024, 256), bf), mk=V((T, 16), f32),
        q=V((T, D), bf), k=V((T, D), bf), v=V((T, D), bf), ab=V((T, 1024), bf), c=V((T, D), bf),
        n1h=V((T, D), f32), n1b=V((T, D), bf), g=V((T, FFW), bf), df=V((T, FFW), bf),
        dz=V((T, D), bf), dr2=V((T, D), f32), b1=V((1, FFW), f32), ib=V(picks, bf),
    )


def compute(x, cot, idx, vec, wa, w1, w2):
    T, D = x.shape
    FFW = 4 * D
    sc = scratch_of(T, D, FFW, (idx.shape[0] * idx.shape[1], idx.shape[2]))
    ins = ["x", "cot", "idx", "vec", "wa", "w1", "w2"]
    outs = dict(
        y=SDS((T, D), bf), dx=SDS((T, D), bf), ga=SDS(wa.shape, bf), g1=SDS(w1.shape, bf), g2=SDS(w2.shape, bf),
        gv=SDS((8, D), f32), gb1=SDS((1, FFW), f32),
    )
    names = ins + list(outs) + list(sc)

    def kern(*refs):
        R = dict(zip(names, refs))
        R["db"] = R["dz"]
        p0(R, lax.axis_index("chan") * (T // L))
        p1(R)
        p2_inner(R)
        p2_outer(R)
        p3_w2(R)
        p2_back(R)
        p3_w1(R)
        grad_attn(R, 3, "c", "db")
        p4(R)
        for i, n in enumerate(("q", "k", "v")):
            grad_attn(R, i, "x", n)

    vm = pl.BlockSpec(memory_space=pltpu.VMEM)
    return pl.pallas_call(
        kern, out_shape=list(outs.values()), in_specs=[vm] * len(ins), out_specs=[vm] * len(outs),
        scratch_shapes=list(sc.values()), compiler_params=pltpu.CompilerParams(vmem_limit_bytes=63 << 20),
    )(x, cot, idx, vec, wa, w1, w2)


MESH = pl.DeviceIdType.MESH
CH = 192


class Copies:
    def __init__(self, ss, rs):
        self.ss, self.rs, self.n = ss, rs, 0
        self.sent = []

    def ids(self, count):
        first = self.n
        self.n += count
        return first

    def make(self, i, src, dst, peer):
        return pltpu.make_async_remote_copy(
            src_ref=src, dst_ref=dst, send_sem=self.ss.at[i], recv_sem=self.rs.at[i], device_id=peer,
            device_id_type=MESH,
        )


N_SEM = 256
N_LOC = 16


def lamb_update(w, g, m, v):
    m2 = beta_first * m + (1.0 - beta_first) * g
    v2 = beta_second * v + (1.0 - beta_second) * g * g
    r = m2 / (1.0 - beta_first**STEP) / (jnp.sqrt(v2 / (1.0 - beta_second**STEP)) + epsilon) + weight_decay * w
    return m2, v2, r


def row_squares(v):
    return jnp.sum(v * v, axis=1, keepdims=True)


def mega(inputs, cotangent, idx, vec, aw, am, av, fw, fm, fv):
    T = inputs.shape[0] // 4
    D = vec.shape[1]
    FFW = 4 * D
    NC = T // CH
    V = pltpu.VMEM
    ins = ["xin", "cin", "idx", "vec", "aw", "am", "av", "fw", "fm", "fv"]
    outs = dict(
        yo=SDS(inputs.shape, bf), dxo=SDS(inputs.shape, bf), oa=SDS(aw.shape, f32), of=SDS(fw.shape, f32),
        ov=SDS((12, D), f32), sq=SDS((8, 128), f32),
    )
    sc = scratch_of(T, D, FFW, (idx.shape[0] * idx.shape[1], idx.shape[2]))
    sc.update(
        x=V((T, D), bf), cot=V((T, D), bf), wa=V((4, 4, NZ, 2, 16, D), bf), w1=V((4, NZ, 2, 16, FFW), bf),
        w2=V((4, NZ, 2, 64, D), bf), ga=V((4, 4, NZ, 2, 16, D), bf), g1=V((4, NZ, 2, 16, FFW), bf),
        g2=V((4, NZ, 2, 64, D), bf), gv=V((8, D), f32), gb1=V((1, FFW), f32),
        ra0=V((4, 4, NZ, 16, D), bf), r10=V((4, NZ, 16, FFW), bf), r20=V((4, NZ, 64, D), bf),
        rax=V((4, 3, NZ, 16, D), bf), raz=V((4, 3, 16, D), bf),
        r1z=V((3, 4, 16, FFW), bf), r1x=V((3, 16, FFW), bf),
        r2z=V((3, 4, 64, D), bf), r2x=V((3, 64, D), bf),
        va=V((16, D), f32), vb=V((16, D), f32), vx=V((4, 16, D), f32), vz=V((NZ, 16, D), f32),
        sh_a=V((4, 16, D), bf), sh_1=V((16, FFW), bf), sh_2=V((64, D), bf), rows=V((64, FFW), f32),
        qa=V((8, 128), f32), qb=V((8, 128), f32), qx=V((4, 8, 128), f32), qz=V((NZ, 8, 128), f32),
        ham=V(am.shape, f32), hav=V(av.shape, f32), hfm=V(fm.shape, f32), hfv=V(fv.shape, f32),
        ss=pltpu.SemaphoreType.DMA((N_SEM,)), rs=pltpu.SemaphoreType.DMA((N_SEM,)),
        ls=pltpu.SemaphoreType.DMA((N_LOC,)),
    )
    names = ins + list(outs) + list(sc)

    def kern(*refs):
        R = dict(zip(names, refs))
        R["y"] = R["cot"]
        R["dx"] = R["c"]
        R["db"] = R["dz"]
        ch = lax.axis_index("chan")
        ro = lax.axis_index("rows")
        z = ro // 2
        c = ro % 2
        o = 1 - c
        px = [(ch ^ d, ro) for d in (1, 2, 3)]
        pz = [(ch, (z ^ d) * 2 + c) for d in (1, 2, 3)]
        pc = (ch, z * 2 + o)
        middle = jnp.logical_or(z == 1, z == 2)
        C = Copies(R["ss"], R["rs"])
        ls = R["ls"]

        def rows_in(src, dst, first):
            def cp(k, d):
                return C.make(
                    first + k * 3 + d - 1, src.at[pl.ds((ch ^ d) * T + k * CH, CH), :],
                    dst.at[pl.ds(k * CH, CH), pl.ds(pl.multiple_of(ch * 128, 128), 128)], px[d - 1],
                )
            return cp

        def rows_out(src, dst, first):
            def cp(k, d):
                return C.make(
                    first + k * 3 + d - 1,
                    src.at[pl.ds(k * CH, CH), pl.ds(pl.multiple_of((ch ^ d) * 128, 128), 128)],
                    dst.at[pl.ds(ch * T + k * CH, CH), :], px[d - 1],
                )
            return cp

        x_cp = rows_in(R["xin"], R["x"], C.ids(3 * NC))
        c_cp = rows_in(R["cin"], R["cot"], C.ids(3 * NC))
        y_cp = rows_out(R["y"], R["yo"], C.ids(3 * NC))
        dx_cp = rows_out(R["dx"], R["dxo"], C.ids(3 * NC))
        DS = (1, 2, 3)
        own = pl.ds(pl.multiple_of(ch * 128, 128), 128)
        x_loc = pltpu.make_async_copy(R["xin"].at[pl.ds(ch * T, T), :], R["x"].at[:, own], ls.at[0])
        c_loc = pltpu.make_async_copy(R["cin"].at[pl.ds(ch * T, T), :], R["cot"].at[:, own], ls.at[1])
        y_loc = pltpu.make_async_copy(R["y"].at[:, own], R["yo"].at[pl.ds(ch * T, T), :], ls.at[2])
        dx_loc = pltpu.make_async_copy(R["dx"].at[:, own], R["dxo"].at[pl.ds(ch * T, T), :], ls.at[3])

        class Gather:
            def __init__(self, shard, loc, place, sets):
                ia, ib, ic, iw = C.ids(3), C.ids(3), C.ids(4), C.ids(1)
                self.loc = pltpu.make_async_copy(shard, place(ch, z, c), ls.at[loc])
                self.plane = [C.make(ia + d - 1, shard, place(ch, z, c), px[d - 1]) for d in DS]
                self.chain = [C.make(ib + d - 1, sets(z, c), sets(z, c), pz[d - 1]) for d in DS]
                self.onward = pltpu.make_async_remote_copy(
                    src_ref=sets(z ^ 2, c), dst_ref=sets(z ^ 2, c), send_sem=C.ss.at[iw], recv_sem=C.rs.at[ib + 2],
                    device_id=pz[0], device_id_type=MESH,
                )
                self.core = [C.make(ic + d, sets(z ^ d, c), sets(z ^ d, c), pc) for d in range(4)]

            def start(self):
                for cp in self.plane:
                    cp.start()
                self.loc.start()

            def along(self):
                self.loc.wait()
                for cp in self.plane:
                    cp.wait_recv()
                for cp in self.chain[:2]:
                    cp.start()

                @pl.when(middle)
                def _():
                    self.chain[2].start()

                self.core[0].start()

            def near(self):
                self.chain[0].wait_recv()
                self.core[1].start()
                self.chain[1].wait_recv()

                @pl.when(middle)
                def _():
                    self.onward.start()

                self.core[2].start()

            def far(self):
                self.chain[2].wait_recv()
                self.core[3].start()

            def arrive(self):
                for cp in self.core:
                    cp.wait_recv()

            def finish(self):
                for cp in self.plane + self.chain[:2] + self.core:
                    cp.wait_send()

                @pl.when(middle)
                def _():
                    self.chain[2].wait_send()
                    self.onward.wait_send()

        class GatherZ:
            def __init__(self, shard, loc, place, sets):
                ia, ib, ic = C.ids(3), C.ids(12), C.ids(4)
                self.loc = pltpu.make_async_copy(shard, place(ch, z, c), ls.at[loc])
                self.chain = [C.make(ia + d - 1, shard, place(ch, z, c), pz[d - 1]) for d in DS]
                self.plane = [
                    [
                        C.make(ib + e * 3 + d - 1, place(ch, z ^ e, c) if e else shard, place(ch, z ^ e, c), px[d - 1])
                        for d in DS
                    ]
                    for e in range(4)
                ]
                self.core = [C.make(ic + d, sets(ch ^ d, c), sets(ch ^ d, c), pc) for d in range(4)]

            def start(self):
                for cp in self.chain + self.plane[0]:
                    cp.start()
                self.loc.start()

            def along(self):
                for e in DS:
                    self.chain[e - 1].wait_recv()
                    for cp in self.plane[e]:
                        cp.start()
                self.loc.wait()
                self.core[0].start()

            def near(self):
                for d in DS:
                    for e in range(4):
                        self.plane[e][d - 1].wait_recv()
                    self.core[d].start()

            def arrive(self):
                for cp in self.core:
                    cp.wait_recv()

            def finish(self):
                for cp in sum(self.plane, []) + self.chain + self.core:
                    cp.wait_send()

        wa, w1, w2 = R["wa"], R["w1"], R["w2"]
        A2, LO, HI = pl.ds(0, 2), pl.ds(0, 32), pl.ds(32, 32)
        sa, s1, s2 = R["sh_a"], R["sh_1"], R["sh_2"]
        GA = GatherZ(sa.at[A2], 4, lambda a, b, e: wa.at[A2, a, b, e], lambda a, e: wa.at[A2, a, :, e])
        GV = Gather(sa.at[2], 9, lambda a, b, e: wa.at[2, a, b, e], lambda b, e: wa.at[2, :, b, e])
        GO = Gather(sa.at[3], 5, lambda a, b, e: wa.at[3, a, b, e], lambda b, e: wa.at[3, :, b, e])
        G1 = Gather(s1, 6, lambda a, b, e: w1.at[a, b, e], lambda b, e: w1.at[:, b, e])
        G2 = Gather(s2.at[LO], 7, lambda a, b, e: w2.at[a, b, e, LO], lambda b, e: w2.at[:, b, e, LO])
        G3 = GatherZ(s2.at[HI], 8, lambda a, b, e: w2.at[a, b, e, HI], lambda a, e: w2.at[a, :, e, HI])

        class Scatter:
            def __init__(self, g, out, b0, bx, bz, plane_first):
                i0, i1, i2 = C.ids(1), C.ids(3), C.ids(3)
                self.g, self.out, self.b0, self.bx, self.bz, self.plane_first = g, out, b0, bx, bz, plane_first
                self.s0 = C.make(i0, g.at[:, :, o], b0, pc)
                if plane_first:
                    self.s1 = [C.make(i1 + d - 1, g.at[ch ^ d, :, c], bx.at[d - 1], px[d - 1]) for d in DS]
                    self.s2 = [C.make(i2 + d - 1, g.at[ch, z ^ d, c], bz.at[d - 1], pz[d - 1]) for d in DS]
                else:
                    self.s1 = [C.make(i1 + d - 1, g.at[:, z ^ d, c], bz.at[d - 1], pz[d - 1]) for d in DS]
                    self.s2 = [C.make(i2 + d - 1, g.at[ch ^ d, z, c], bx.at[d - 1], px[d - 1]) for d in DS]

            def begin(self):
                self.s0.start()

            def one(self):
                self.s0.wait_recv()
                g = self.g

                @pl.loop(0, 4)
                def _(j):
                    g[j, :, c] = (g[j, :, c].astype(f32) + self.b0[j].astype(f32)).astype(bf)

                for cp in self.s1:
                    cp.start()

            def two(self):
                for cp in self.s1:
                    cp.wait_recv()
                g = self.g
                b = self.bx if self.plane_first else self.bz

                @pl.loop(0, 4)
                def _(j):
                    t = b[0, j].astype(f32) + b[1, j].astype(f32) + b[2, j].astype(f32)
                    if self.plane_first:
                        g[ch, j, c] = (g[ch, j, c].astype(f32) + t).astype(bf)
                    else:
                        g[j, z, c] = (g[j, z, c].astype(f32) + t).astype(bf)

                for cp in self.s2:
                    cp.start()

            def three(self):
                for cp in self.s2:
                    cp.wait_recv()
                b = self.bz if self.plane_first else self.bx
                t = b[0].astype(f32) + b[1].astype(f32) + b[2].astype(f32)
                t = self.g[ch, z, c].astype(f32) + t
                ref, row = self.out
                n = t.shape[1]
                for k in range(t.shape[0]):
                    ref[row : row + 1, k * n : (k + 1) * n] = t[k : k + 1, :]

            def finish(self):
                for cp in [self.s0] + self.s1 + self.s2:
                    cp.wait_send()

        S1 = Scatter(R["g1"], (R["of"], 0), R["r10"], R["r1x"], R["r1z"], False)
        S2 = Scatter(R["g2"], (R["of"], 1), R["r20"], R["r2x"], R["r2z"], False)
        SA = [Scatter(R["ga"].at[0], (R["oa"], 0), R["ra0"].at[0], R["raz"].at[0], R["rax"].at[0], False)] + [
            Scatter(R["ga"].at[i], (R["oa"], i), R["ra0"].at[i], R["rax"].at[i], R["raz"].at[i], True) for i in (1, 2, 3)
        ]
        va, vb, vx, vz = R["va"], R["vb"], R["vx"], R["vz"]
        iv = C.ids(7)
        v0 = C.make(iv, va, vb, pc)
        v1 = [C.make(iv + d, vx.at[ch], vx.at[ch], px[d - 1]) for d in DS]
        v2 = [C.make(iv + 3 + d, vz.at[z], vz.at[z], pz[d - 1]) for d in DS]
        qa, qb, qx, qz = R["qa"], R["qb"], R["qx"], R["qz"]
        iq = C.ids(7)
        q0 = C.make(iq, qa, qb, pc)
        q1 = [C.make(iq + d, qx.at[ch], qx.at[ch], px[d - 1]) for d in DS]
        q2 = [C.make(iq + 3 + d, qz.at[z], qz.at[z], pz[d - 1]) for d in DS]
        assert C.n <= N_SEM

        bar = pltpu.get_barrier_semaphore()
        for peer in px + pz + [pc]:
            pl.semaphore_signal(bar, inc=1, device_id=peer, device_id_type=MESH)
        held = [pltpu.make_async_copy(R[n], R["h" + n], ls.at[10 + i]) for i, n in enumerate(("am", "av", "fm", "fv"))]
        for cp in held:
            cp.start()
        x_loc.start()
        c_loc.start()
        tmp = R["rows"]

        def split(src, row, count, n):
            for k in range(count):
                tmp[k : k + 1, 0:n] = src[row : row + 1, k * n : (k + 1) * n]
            return tmp[0:count, 0:n].astype(bf)

        for i in range(4):
            R["sh_a"][i] = split(R["aw"], i, 16, D)
        R["sh_1"][...] = split(R["fw"], 0, 16, FFW)
        R["sh_2"][...] = split(R["fw"], 1, 64, D)
        pl.semaphore_wait(bar, 7)

        GA.start()
        GV.start()
        for d in DS:
            x_cp(0, d).start()
        GO.start()
        G1.start()
        GV.along()
        GA.along()
        G3.start()
        G2.start()

        @pl.loop(1, NC)
        def _(k):
            for d in DS:
                x_cp(k, d).start()

        GO.along()
        G1.along()
        G2.along()
        G3.along()
        p0(R, ch * (T // L))
        GV.near()
        GA.near()
        GO.near()
        GV.far()
        GO.far()
        GA.arrive()
        GV.arrive()
        GO.arrive()
        x_loc.wait()

        def hook1(i):
            for k in range(TM1 // CH):
                for d in DS:
                    x_cp(i * (TM1 // CH) + k, d).wait_recv()
                for d in DS:
                    c_cp(i * (TM1 // CH) + k, d).start()

            @pl.when(i == 2)
            def _():
                G1.near()

            @pl.when(i == 3)
            def _():
                G1.far()

        p1(R, hook1)
        G1.arrive()
        G3.near()
        G2.near()
        p2_inner(R)
        G2.far()
        c_loc.wait()
        G3.arrive()
        G2.arrive()

        def hook2(i):
            for k in range(TM2 // CH):
                for d in DS:
                    c_cp(i * (TM2 // CH) + k, d).wait_recv()

        def done2(i):
            for k in range(TM2 // CH):
                for d in DS:
                    y_cp(i * (TM2 // CH) + k, d).start()

        p2_outer(R, hook2, done2)
        y_loc.start()
        p3_w2(R)
        S2.begin()

        def hook3(i):
            @pl.when(i == 1)
            def _():
                S2.one()

        p2_back(R, hook3)
        p3_w1(R)
        S1.begin()
        grad_attn(R, 3, "c", "db")
        S1.one()
        SA[3].begin()

        def hook4(i):
            @pl.when(i == 1)
            def _():
                SA[3].one()

            @pl.when(i == 2)
            def _():
                S2.two()

        def done4(i):
            for k in range(TM1 // CH):
                for d in DS:
                    dx_cp(i * (TM1 // CH) + k, d).start()

        p4(R, hook4, done4)
        dx_loc.start()
        va[4:12, :] = R["gv"][...]
        for j in range(4):
            va[j : j + 1, :] = R["gb1"][:, j * D : (j + 1) * D]
        va[12:16, :] = jnp.zeros((4, D), f32)
        v0.start()
        grad_attn(R, 0, "x", "q")
        SA[0].begin()
        v0.wait_recv()
        vx[ch] = va[...] + vb[...]
        for cp in v1:
            cp.start()
        grad_attn(R, 1, "x", "k")
        SA[1].begin()
        SA[0].one()
        grad_attn(R, 2, "x", "v")
        SA[2].begin()
        SA[1].one()
        SA[3].two()
        SA[2].one()
        S2.three()
        S1.two()
        for cp in v1:
            cp.wait_recv()
        vz[z] = vx[0] + vx[1] + vx[2] + vx[3]
        for cp in v2:
            cp.start()
        SA[3].three()
        SA[0].two()
        SA[1].two()
        SA[2].two()
        S1.three()
        for cp in held:
            cp.wait()
        qa[...] = jnp.zeros_like(qa)
        qa[0:4, 0:1] = row_squares(R["aw"][...])
        qa[4:6, 0:1] = row_squares(R["fw"][...])
        qa[4:6, 1:2] = row_squares(lamb_update(R["fw"][...], R["of"][...], R["hfm"][...], R["hfv"][...])[2])
        for cp in v2:
            cp.wait_recv()
        tot = vz[0] + vz[1] + vz[2] + vz[3]
        R["ov"][...] = tot[0:12, :]
        for i in range(3):
            SA[i].three()
        qa[0:4, 1:2] = row_squares(lamb_update(R["aw"][...], R["oa"][...], R["ham"][...], R["hav"][...])[2])
        q0.start()
        q0.wait_recv()
        qx[ch] = qa[...] + qb[...]
        for cp in q1:
            cp.start()
        for cp in q1:
            cp.wait_recv()
        qz[z] = qx[0] + qx[1] + qx[2] + qx[3]
        for cp in q2:
            cp.start()

        @pl.loop(0, NC)
        def _(k):
            for d in DS:
                y_cp(k, d).wait_recv()
                dx_cp(k, d).wait_recv()
                x_cp(k, d).wait_send()
                c_cp(k, d).wait_send()
                y_cp(k, d).wait_send()
                dx_cp(k, d).wait_send()

        y_loc.wait()
        dx_loc.wait()
        for t in (GA, GV, GO, G1, G2, G3, S1, S2, *SA):
            t.finish()
        for cp in q2:
            cp.wait_recv()
        R["sq"][...] = qz[0] + qz[1] + qz[2] + qz[3]
        for cp in [v0, q0] + v1 + v2 + q1 + q2:
            cp.wait_send()

    vm = pl.BlockSpec(memory_space=pltpu.VMEM)
    an = pl.BlockSpec(memory_space=pl.ANY)
    return pl.pallas_call(
        kern, out_shape=list(outs.values()), in_specs=[an, an, vm, vm, vm, an, an, vm, an, an],
        out_specs=[an, an, vm, vm, vm, vm], scratch_shapes=list(sc.values()),
        compiler_params=pltpu.CompilerParams(
            vmem_limit_bytes=63 << 20, collective_id=0, has_side_effects=True
        ),
    )(inputs, cotangent, idx, vec, aw, am, av, fw, fm, fv)


def finish(yi, dxi, sets, squares):
    shapes = [SDS(yi.shape, bf), SDS(dxi.shape, bf)]
    flat = []
    for w, g, m, v in sets:
        flat += [w, g, m, v]
        shapes += [SDS(w.shape, f32)] * 4
    shapes += [SDS(sets[0][0].shape, bf), SDS(sets[1][0].shape, bf), SDS((2, 6), f32)]
    n = len(flat)

    def kern(*refs):
        ya, xa, sq = refs[0], refs[1], refs[2]
        src = refs[3 : 3 + n]
        yb, xb = refs[3 + n : 5 + n]
        dst = refs[5 + n : 5 + 2 * n]
        low_a, low_f, norms, hold, sems = refs[5 + 2 * n :]
        part = ya.shape[0] // 4
        load = []
        save = []
        for k in range(8):
            rows = pl.ds((k % 4) * part, part)
            src_ref, dst_ref = ((ya, yb), (xa, xb))[k // 4]
            load.append(pltpu.make_async_copy(src_ref.at[rows], hold.at[k], sems.at[k]))
            save.append(pltpu.make_async_copy(hold.at[k], dst_ref.at[rows], sems.at[8 + k]))
        for cp in load:
            cp.start()
        root = jnp.sqrt(sq[...])
        norms[...] = jnp.transpose(root)[0:2, 0:6]
        for k in range(8):
            load[k].wait()
            save[k].start()
        ratio = root[:, 0:1] * lax.rsqrt(sq[:, 1:2] + epsilon)
        for k in range(3):
            w, g, m, v = [r[...] for r in src[4 * k : 4 * k + 4]]
            m2, v2, r = lamb_update(w, g, m, v)
            if k == 2:
                rate = jnp.sqrt(row_squares(w)) * lax.rsqrt(row_squares(r) + epsilon)
            else:
                rate = ratio[0:4] if k == 0 else ratio[4:6]
            new = w - learn_rate * rate * r
            for ref, val in zip(dst[4 * k : 4 * k + 4], (new, g, m2, v2)):
                ref[...] = val
            if k < 2:
                (low_a, low_f)[k][...] = new.astype(bf)
        for cp in save:
            cp.wait()

    vm = pl.BlockSpec(memory_space=pltpu.VMEM)
    an = pl.BlockSpec(memory_space=pl.ANY)
    return pl.pallas_call(
        kern, out_shape=shapes, in_specs=[an, an] + [vm] * (1 + n), out_specs=[an, an] + [vm] * (n + 3),
        scratch_shapes=[
            pltpu.VMEM((8, yi.shape[0] // 4, yi.shape[1]), bf), pltpu.SemaphoreType.DMA((16,)),
        ],
        compiler_params=pltpu.CompilerParams(vmem_limit_bytes=63 << 20),
    )(yi, dxi, squares, *flat)


def native(inputs, cotangent, idx, vec, aw, am, av, fw, fm, fv):
    axes = ("chan", "rows")
    D = vec.shape[1]
    x = lax.all_to_all(inputs, "chan", split_axis=0, concat_axis=1, tiled=True)
    cot = lax.all_to_all(cotangent, "chan", split_axis=0, concat_axis=1, tiled=True)
    wa = lax.all_gather(aw.astype(bf), axes, axis=1, tiled=True)
    wf = lax.all_gather(fw.astype(bf), axes, axis=1, tiled=True)
    y, dx, ga, g1, g2, gv, gb1 = compute(
        x, cot, idx, vec, wa.reshape(4, 4, NZ, 2, 16, D), wf[0].reshape(4, NZ, 2, 16, -1), wf[1].reshape(4, NZ, 2, 64, D)
    )
    yo = lax.all_to_all(y, "chan", split_axis=1, concat_axis=0, tiled=True)
    dxo = lax.all_to_all(dx, "chan", split_axis=1, concat_axis=0, tiled=True)
    ga = ga.reshape(4, -1).astype(f32)
    gf = jnp.stack([g1.reshape(-1), g2.reshape(-1)]).astype(f32)
    ga = lax.psum_scatter(ga, axes, scatter_dimension=1, tiled=True)
    gf = lax.psum_scatter(gf, axes, scatter_dimension=1, tiled=True)
    gv = lax.psum(jnp.concatenate([gb1.reshape(4, D), gv], axis=0), axes)
    part = []
    for w, g, m, v in ((aw, ga, am, av), (fw, gf, fm, fv)):
        part.append(jnp.concatenate([row_squares(w), row_squares(lamb_update(w, g, m, v)[2])], axis=1))
    squares = jnp.zeros((8, 128), f32).at[0:6, 0:2].set(lax.psum(jnp.concatenate(part, axis=0), axes))
    return yo, dxo, ga, gf, gv, squares


def step(move, inputs, cotangent, top_index, aw, am, av, fw, fm, fv, vec, vm, vv):
    yo, dxo, ga, gf, gv, squares = move(inputs, cotangent, jnp.transpose(top_index, (2, 1, 0)), vec, aw, am, av, fw, fm, fv)
    sets = ((aw, ga, am, av), (fw, gf, fm, fv), (vec, gv, vm, vv))
    r = finish(yo, dxo, sets, squares)
    aw2, ga, am2, av2, fw2, gf, fm2, fv2, vec2, gv, vm2, vv2 = r[2:14]
    return r[0], r[1], ga, gf, gv, am2, av2, fm2, fv2, vm2, vv2, aw2, fw2, vec2, r[14], r[15], r[16].T


def solution(mesh):
    small = mesh.shape["chan"] == 4 and mesh.shape["rows"] == 2 * NZ
    local = functools.partial(step, mega if small else native)
    in_specs = (
        P("rows", "chan"),
        P("rows", "chan"),
        P("rows", None, None),
        P(None, ("chan", "rows")),
        P(None, ("chan", "rows")),
        P(None, ("chan", "rows")),
        P(None, ("chan", "rows")),
        P(None, ("chan", "rows")),
        P(None, ("chan", "rows")),
        P(),
        P(),
        P(),
    )
    out_specs = (
        P("rows", "chan"),
        P("rows", "chan"),
        P(None, ("chan", "rows")),
        P(None, ("chan", "rows")),
        P(),
        P(None, ("chan", "rows")),
        P(None, ("chan", "rows")),
        P(None, ("chan", "rows")),
        P(None, ("chan", "rows")),
        P(),
        P(),
        P(None, ("chan", "rows")),
        P(None, ("chan", "rows")),
        P(),
        P(None, ("chan", "rows")),
        P(None, ("chan", "rows")),
        P(),
    )
    return jax.shard_map(local, mesh=mesh, in_specs=in_specs, out_specs=out_specs, check_vma=False)
```
